256 devices in a mesh: dp: 4 (over x), seq: 16 (over z, core), tensor: 4 (over y).
Axes of the slice: x: 4, y: 4, z: 8, core: 2. Of those that a mesh axis runs over, the one named last changes fastest.
Arguments:
- feature_in: bfloat16 [16, 2048, 512], P('dp', 'seq', 'tensor'), may hold values from -6 to 6
- conv_weight: bfloat16 [2, 512, 512], P(None, 'tensor'), may hold values from -0.1875 to 0.1875
- proj_weight: bfloat16 [512, 1920], P(None, 'tensor'), may hold values from -0.25 to 0.25
- mask_embed: bfloat16 [1920], P('tensor'), may hold values from -5 to 5
- pos_weight: bfloat16 [128, 16, 120, 120], P(('dp', 'seq'), 'tensor'), may hold values from -0.046875 to 0.046875
- final_weight: bfloat16 [1920, 1024], P('tensor'), may hold values from -0.125 to 0.125
- codebook: bfloat16 [2, 320, 512], replicated, may hold values from -6 to 6
- quant_weight: bfloat16 [1024, 1024], replicated, may hold values from -0.1875 to 0.1875
- mask_starts: int32 [16, 66], P('dp'), may hold values from 0 to 1014
- code_choice: int32 [16, 1024, 2], P(('dp', 'tensor'), 'seq'), may hold values from 0 to 319
- negative_ids: int32 [16, 1024, 100], P(('dp', 'tensor'), 'seq'), may hold values from 0 to 1023, as said below
Outputs:
- frame_loss: float32 [16, 1024], P(('dp', 'tensor'), 'seq')
The draws below stay inside these ranges and needn't reach their ends.
Inputs may be any that keep to these rules, and one draw needn't show every extreme that they name: `negative_ids`: each entry names a frame of the same utterance other than the frame itself.
All inputs are finite; a program needn't handle non-finite values.
Results may differ from the reference program's by a relative error of at most 0.00065.
Values may be sent and summed in bfloat16 or wider, within the bound.
A program may use at most 128 MiB of HBM per device.

```python
import jax
import jax.numpy as jnp
from jax import lax

CH = 512
WIDTH = 1920
GROUPS = 16
KERNEL = 128
CODE_DIM = 1024
ENTRIES = 320
QGROUPS = 2
NEGS = 100
MASK_LEN = 10
UTT = 16
FRAMES = 1024
STARTS = 66


def draw_negative_ids(key, part):
    offsets = jax.random.randint(key, (UTT, FRAMES, NEGS), 1, FRAMES, dtype=jnp.int32)
    frame_index = jnp.arange(FRAMES, dtype=jnp.int32)[None, :, None]
    return (frame_index + offsets) % FRAMES


def with_ends(values, rng, low, largest):
    place = [jax.random.randint(jax.random.fold_in(rng, axis), (), 0, length) for axis, length in enumerate(values.shape)]
    widest = values.shape.index(max(values.shape))
    neighbour = place[:widest] + [(place[widest] + 1) % values.shape[widest]] + place[widest + 1:]
    return values.at[tuple(place)].set(low).at[tuple(neighbour)].set(largest)


def levels(stream_key, dims, cuts, least, high):
    factor_of = 1.0
    for dim, shards_of in cuts:
        draws = jax.random.uniform(jax.random.fold_in(jax.random.fold_in(stream_key, 6), dim), (shards_of,), jnp.float32, least / len(cuts), high / len(cuts))
        factor_of = factor_of * jnp.repeat(jnp.exp(draws), dims[dim] // shards_of).reshape((-1,) + (1,) * (len(dims) - 1 - dim))
    return factor_of


def noise(own_key, shape, spread, bound, cuts=(), kind=jnp.bfloat16):
    array = spread * jax.random.normal(own_key, shape, jnp.float32)
    if cuts:
        array = array * levels(own_key, shape, cuts, -0.22, 0.18)
    return jnp.clip(array, -bound, bound).astype(kind)


def setup_inputs(seed: int = 0) -> dict:
    streams_of = jax.random.split(jax.random.key(seed), 12)
    feature_in = noise(streams_of[0], (UTT, 2 * FRAMES, CH), 1.0, 6.0, ((0, 4), (1, 16), (2, 4)))
    conv_weight = noise(streams_of[1], (2, CH, CH), (2 * CH) ** -0.5, 0.1875, ((1, 4),))
    proj_weight = noise(streams_of[2], (CH, WIDTH), CH ** -0.5, 0.25, ((1, 4),))
    mask_embed = noise(streams_of[3], (WIDTH,), 1.0, 5.0, ((0, 4),))
    pos_weight = noise(streams_of[4], (KERNEL, GROUPS, WIDTH // GROUPS, WIDTH // GROUPS), (KERNEL * WIDTH // GROUPS) ** -0.5, 0.046875, ((0, 64), (1, 4)))
    final_weight = noise(streams_of[5], (WIDTH, CODE_DIM), WIDTH ** -0.5, 0.125, ((0, 4),))
    codebook = noise(streams_of[6], (QGROUPS, ENTRIES, CODE_DIM // QGROUPS), 1.0, 6.0)
    quant_weight = noise(streams_of[7], (CODE_DIM, CODE_DIM), CODE_DIM ** -0.5, 0.1875)
    mask_starts = with_ends(jax.random.randint(streams_of[8], (UTT, STARTS), 0, FRAMES - MASK_LEN + 1), jax.random.fold_in(streams_of[8], 1), 0, FRAMES - MASK_LEN).astype(jnp.int32)
    code_choice = with_ends(jax.random.randint(streams_of[9], (UTT, FRAMES, QGROUPS), 0, ENTRIES), jax.random.fold_in(streams_of[9], 1), 0, ENTRIES - 1).astype(jnp.int32)
    negative_ids = draw_negative_ids(jax.random.fold_in(streams_of[11], 71), 0)
    return dict(feature_in=feature_in, conv_weight=conv_weight, proj_weight=proj_weight, mask_embed=mask_embed, pos_weight=pos_weight, final_weight=final_weight, codebook=codebook, quant_weight=quant_weight, mask_starts=mask_starts, code_choice=code_choice, negative_ids=negative_ids)


ln_eps = 1e-05
norm_eps = 1e-06
logit_temp = 0.1

def norm_gelu(conv_total):
    row_mean = lax.optimization_barrier(jnp.mean(conv_total, axis=-1, keepdims=True))
    row_square = lax.optimization_barrier(jnp.mean(conv_total * conv_total, axis=-1, keepdims=True))
    normed = (conv_total - row_mean) * lax.rsqrt(row_square - row_mean * row_mean + ln_eps)
    return jax.nn.gelu(normed, approximate=False).astype(jnp.bfloat16)

def make_targets(code_choice, codebook, quant_weight):
    pieces = [codebook[qgroup][code_choice[..., qgroup]] for qgroup in range(codebook.shape[0])]
    codevec = jnp.concatenate(pieces, axis=-1)
    return jnp.dot(codevec, quant_weight, preferred_element_type=jnp.float32).astype(jnp.bfloat16)

def utterance_loss(block):
    context, targets, neg_ids, is_masked = block
    ctx_wide = context.astype(jnp.float32)
    tgt_wide = targets.astype(jnp.float32)
    scores = jnp.einsum('fc,nc->fn', ctx_wide, tgt_wide, precision=lax.Precision.HIGHEST)
    ctx_norm = lax.optimization_barrier(jnp.sum(ctx_wide * ctx_wide, axis=-1))
    tgt_norm = lax.optimization_barrier(jnp.sum(tgt_wide * tgt_wide, axis=-1))
    pos_dot = lax.optimization_barrier(jnp.sum(ctx_wide * tgt_wide, axis=-1))
    neg_dot = jnp.take_along_axis(scores, neg_ids, axis=1)
    neg_norm = tgt_norm[neg_ids]
    positive = pos_dot * lax.rsqrt((ctx_norm + norm_eps) * (tgt_norm + norm_eps)) / logit_temp
    negative = neg_dot * lax.rsqrt((ctx_norm[:, None] + norm_eps) * (neg_norm + norm_eps)) / logit_temp
    frame_loss = jnp.log(jnp.exp(positive) + lax.optimization_barrier(jnp.sum(jnp.exp(negative), axis=-1))) - positive
    return jnp.where(is_masked, frame_loss, jnp.zeros_like(frame_loss))

def reference(feature_in, conv_weight, proj_weight, mask_embed, pos_weight, final_weight, codebook, quant_weight, mask_starts, code_choice, negative_ids):
    utt_count, sample_rows, channels = feature_in.shape
    frame_count = sample_rows // 2
    frame_pairs = feature_in.reshape(utt_count, frame_count, 2 * channels)
    conv_total = jnp.dot(frame_pairs, conv_weight.reshape(2 * channels, channels), preferred_element_type=jnp.float32)
    features = norm_gelu(conv_total)
    projected = jnp.dot(features, proj_weight, preferred_element_type=jnp.float32).astype(jnp.bfloat16)
    positions = jnp.arange(frame_count, dtype=jnp.int32)[None, :, None]
    starts = mask_starts[:, None, :]
    masked = jnp.any((positions >= starts) & (positions < starts + MASK_LEN), axis=-1)
    hidden = jnp.where(masked[..., None], mask_embed[None, None, :], projected)
    lhs_field = hidden.astype(jnp.float32).transpose(0, 2, 1)
    kernel_oik = pos_weight.astype(jnp.float32).transpose(1, 3, 2, 0).reshape(WIDTH, WIDTH // GROUPS, KERNEL)
    conv_out = lax.conv_general_dilated(lhs_field, kernel_oik, (1,), [(KERNEL // 2, KERNEL // 2 - 1)], dimension_numbers=('NCH', 'OIH', 'NCH'), feature_group_count=GROUPS, precision=lax.Precision.HIGHEST)
    conv_out = conv_out.transpose(0, 2, 1)
    mixed = (hidden.astype(jnp.float32) + jax.nn.gelu(conv_out, approximate=False)).astype(jnp.bfloat16)
    context = jnp.dot(mixed, final_weight, preferred_element_type=jnp.float32).astype(jnp.bfloat16)
    targets = make_targets(code_choice, codebook, quant_weight)
    return lax.map(utterance_loss, (context, targets, negative_ids, masked))
```

```python
import functools

import jax
import jax.numpy as jnp
from jax import lax
from jax.experimental import pallas as pl
from jax.experimental.pallas import tpu as pltpu
from jax.sharding import PartitionSpec as P

KERNEL = 128
MASK_LEN = 10
SHIFTS = 16
LANES = 128


ln_eps = 1e-05
norm_eps = 1e-06
logit_temp = 0.1


def exact_gelu(value):
    return 0.5 * value * (1.0 + lax.erf(value * (0.5**0.5)))


def extended(block, sides, width):
    for axis, dim in sides:
        count = lax.axis_size(axis)
        forward = [(i, i + 1) for i in range(count - 1)]
        backward = [(target, source) for source, target in forward]
        low = lax.ppermute(
            lax.slice_in_dim(block, block.shape[dim] - width, None, axis=dim), axis, forward
        )
        high = lax.ppermute(lax.slice_in_dim(block, 0, width, axis=dim), axis, backward)
        block = jnp.concatenate([low, block, high], axis=dim)
    return block


def make_targets(code_block, codebook, quant_weight):
    entries = codebook.shape[1]
    choices_row = jnp.arange(entries, dtype=jnp.int32)
    pieces = []
    for qgroup in range(codebook.shape[0]):
        onehot = (code_block[..., qgroup, None] == choices_row).astype(jnp.bfloat16)
        pieces.append(
            jnp.dot(onehot, codebook[qgroup], preferred_element_type=jnp.float32).astype(
                jnp.bfloat16
            )
        )
    codevec = jnp.concatenate(pieces, axis=-1)
    return jnp.dot(codevec, quant_weight, preferred_element_type=jnp.float32).astype(jnp.bfloat16)


def conv_body(x_ref, w_ref, fw_ref, o_ref, xf, xc, wc, acc):
    group, step = pl.program_id(0), pl.program_id(1)
    utts, rows, _ = x_ref.shape[1:]
    inner, outer = w_ref.shape[2:]
    frames = rows - KERNEL
    span = frames + SHIFTS
    kept = rows - SHIFTS

    @pl.when((group == 0) & (step == 0))
    def clear():
        wc[...] = jnp.zeros_like(wc)
        o_ref[...] = jnp.zeros_like(o_ref)

    @pl.when(step == 0)
    def shift_copies():
        acc[...] = jnp.zeros_like(acc)

        @pl.loop(0, utts)
        def one(u):
            xf[...] = x_ref[0, u].astype(jnp.float32)
            for j in range(SHIFTS):
                xc[u, :, j * LANES : (j + 1) * LANES] = xf[j : j + kept, :].astype(jnp.bfloat16)

    for half in range(2):
        for j in range(SHIFTS):
            wc[
                j * LANES : j * LANES + inner, half * LANES : half * LANES + outer
            ] = w_ref[half * SHIFTS + j, 0]
    first = pl.multiple_of(step * (2 * SHIFTS), 2 * SHIFTS)
    window = xc[:, pl.ds(first, span), :].reshape(utts * span, SHIFTS * LANES)
    acc[...] += jnp.dot(window, wc[...], preferred_element_type=jnp.float32).reshape(
        utts, span, 2 * LANES
    )

    @pl.when(step == pl.num_programs(1) - 1)
    def finish():
        conv_out = acc[:, :frames, :LANES] + acc[:, SHIFTS:, LANES:]
        own = x_ref[0, :, KERNEL // 2 : KERNEL // 2 + frames, :].astype(jnp.float32)
        mixed = (own + exact_gelu(conv_out)).astype(jnp.bfloat16)
        mixed = mixed.reshape(utts * frames, LANES)[:, :inner]
        o_ref[...] += jnp.dot(mixed, fw_ref[0], preferred_element_type=jnp.float32)


def conv_context(windows, taps, final_weight):
    groups, utts, rows, _ = windows.shape
    count, _, inner, outer = taps.shape
    frames = rows - KERNEL
    span = frames + SHIFTS
    steps = count // (2 * SHIFTS)
    code_dim = final_weight.shape[-1]
    return pl.pallas_call(
        conv_body,
        grid=(groups, steps),
        out_shape=jax.ShapeDtypeStruct((utts * frames, code_dim), jnp.float32),
        in_specs=[
            pl.BlockSpec((1, utts, rows, LANES), lambda g, p: (g, 0, 0, 0)),
            pl.BlockSpec((2 * SHIFTS, 1, inner, outer), lambda g, p: (p, g, 0, 0)),
            pl.BlockSpec((1, inner, code_dim), lambda g, p: (g, 0, 0)),
        ],
        out_specs=pl.BlockSpec((utts * frames, code_dim), lambda g, p: (0, 0)),
        scratch_shapes=[
            pltpu.VMEM((rows, LANES), jnp.float32),
            pltpu.VMEM((utts, rows - SHIFTS, SHIFTS * LANES), jnp.bfloat16),
            pltpu.VMEM((SHIFTS * LANES, 2 * LANES), jnp.bfloat16),
            pltpu.VMEM((utts, span, 2 * LANES), jnp.float32),
        ],
        compiler_params=pltpu.CompilerParams(vmem_limit_bytes=56 * 2**20),
        cost_estimate=pl.CostEstimate(
            flops=2 * utts * frames * count * groups * inner * outer,
            bytes_accessed=taps.size * 2,
            transcendentals=0,
        ),
    )(windows, taps, final_weight)


def loss_body(c_ref, t_ref, own_ref, tn_ref, count_ref, mask_ref, o_ref):
    context = c_ref[...]
    scores = lax.dot_general(
        context, t_ref[...], (((1,), (1,)), ((), ())), preferred_element_type=jnp.float32
    )
    wide = context.astype(jnp.float32)
    own = own_ref[...].astype(jnp.float32)
    ctx_norm = jnp.sum(wide * wide, axis=-1, keepdims=True) + norm_eps
    own_norm = jnp.sum(own * own, axis=-1, keepdims=True) + norm_eps
    pos_dot = jnp.sum(wide * own, axis=-1, keepdims=True)
    positive = pos_dot * lax.rsqrt(ctx_norm * own_norm) / logit_temp
    logits = scores * lax.rsqrt(ctx_norm * (tn_ref[...] + norm_eps)) / logit_temp
    total = jnp.sum(count_ref[...] * jnp.exp(logits), axis=-1, keepdims=True)
    loss = jnp.log(jnp.exp(positive) + total) - positive
    o_ref[...] = jnp.where(mask_ref[...] > 0, loss, 0.0)


def on_device(
    feature_in,
    conv_weight,
    proj_weight,
    mask_embed,
    pos_weight,
    final_weight,
    codebook,
    quant_weight,
    mask_starts,
    code_choice,
    negative_ids,
):
    utt_count, sample_rows, channels = feature_in.shape
    frames = sample_rows // 2
    utt_rows = utt_count // lax.axis_size("tensor")
    seq_count = lax.axis_size("seq")

    all_codes = lax.all_gather(code_choice.reshape(-1), "seq", axis=0, tiled=True)
    all_codes = all_codes.reshape(seq_count * frames, code_choice.shape[-1])
    taps = lax.all_gather(pos_weight, ("dp", "seq"), axis=0, tiled=True)

    frame_pairs = feature_in.reshape(utt_count, frames, 2 * channels)
    conv_term = jnp.dot(
        frame_pairs,
        conv_weight.reshape(2 * channels, conv_weight.shape[2]),
        preferred_element_type=jnp.float32,
    )
    summed = lax.psum(conv_term, "tensor")
    row_mean = jnp.mean(summed, axis=-1, keepdims=True)
    row_square = jnp.mean(summed * summed, axis=-1, keepdims=True)
    normed = (summed - row_mean) * lax.rsqrt(row_square - row_mean * row_mean + ln_eps)
    features = jax.nn.gelu(normed, approximate=False).astype(jnp.bfloat16)
    projected = jnp.dot(features, proj_weight, preferred_element_type=jnp.float32).astype(
        jnp.bfloat16
    )
    positions = (lax.axis_index("seq") * frames + jnp.arange(frames, dtype=jnp.int32))[
        None, :, None
    ]
    starts = mask_starts[:, None, :]
    masked = jnp.any((positions >= starts) & (positions < starts + MASK_LEN), axis=-1)
    hidden = jnp.where(masked[..., None], mask_embed[None, None, :], projected)
    padded = extended(hidden, (("seq", 1),), KERNEL // 2)

    all_targets = make_targets(all_codes, codebook, quant_weight)
    wide_targets = all_targets.astype(jnp.float32)
    tgt_norm = jnp.sum(wide_targets * wide_targets, axis=-1)[None, :]
    own_targets = lax.dynamic_slice_in_dim(
        all_targets, lax.axis_index("seq") * frames, frames, 0
    )
    ids = negative_ids.reshape(frames, negative_ids.shape[-1])
    frame_row = jnp.arange(seq_count * frames, dtype=jnp.int32)
    counts = jnp.sum((ids[:, :, None] == frame_row).astype(jnp.float32), axis=1)
    padded, all_targets, own_targets, tgt_norm, counts = lax.optimization_barrier(
        (padded, all_targets, own_targets, tgt_norm, counts)
    )

    group_count, inner = pos_weight.shape[1], pos_weight.shape[2]
    windows = padded.reshape(utt_count, padded.shape[1], group_count, inner)
    windows = jnp.pad(windows.transpose(2, 0, 1, 3), ((0, 0), (0, 0), (0, 0), (0, LANES - inner)))
    partial = conv_context(
        windows, taps, final_weight.reshape(group_count, inner, final_weight.shape[1])
    )
    context = lax.psum_scatter(partial, "tensor", scatter_dimension=0, tiled=True).astype(
        jnp.bfloat16
    )
    is_masked = lax.dynamic_slice_in_dim(masked, lax.axis_index("tensor") * utt_rows, utt_rows, 0)
    loss = pl.pallas_call(
        loss_body,
        out_shape=jax.ShapeDtypeStruct((utt_rows * frames, 1), jnp.float32),
        compiler_params=pltpu.CompilerParams(vmem_limit_bytes=24 * 2**20),
    )(
        context,
        all_targets,
        own_targets,
        tgt_norm,
        counts,
        is_masked.reshape(utt_rows * frames, 1).astype(jnp.float32),
    )
    return loss.reshape(utt_rows, frames)


def solution(mesh):
    return jax.shard_map(
        on_device,
        mesh=mesh,
        in_specs=(
            P("dp", "seq", "tensor"),
            P(None, "tensor", None),
            P(None, "tensor"),
            P("tensor"),
            P(("dp", "seq"), "tensor", None, None),
            P("tensor", None),
            P(),
            P(),
            P("dp", None),
            P(("dp", "tensor"), "seq", None),
            P(("dp", "tensor"), "seq", None),
        ),
        out_specs=P(("dp", "tensor"), "seq"),
        check_vma=False,
    )
```

```python
import functools

import jax
import jax.numpy as jnp
from jax import lax
from jax.experimental import pallas as pl
from jax.experimental.pallas import tpu as pltpu
from jax.sharding import PartitionSpec as P

KERNEL = 128
MASK_LEN = 10
SHIFTS = 16
LANES = 128


ln_eps = 1e-05
norm_eps = 1e-06
logit_temp = 0.1


def exact_gelu(value):
    return 0.5 * value * (1.0 + lax.erf(value * (0.5**0.5)))


def make_targets(code_block, codebook, quant_weight):
    entries = codebook.shape[1]
    choices_row = jnp.arange(entries, dtype=jnp.int32)
    pieces = []
    for qgroup in range(codebook.shape[0]):
        onehot = (code_block[..., qgroup, None] == choices_row).astype(jnp.bfloat16)
        pieces.append(
            jnp.dot(onehot, codebook[qgroup], preferred_element_type=jnp.float32).astype(
                jnp.bfloat16
            )
        )
    codevec = jnp.concatenate(pieces, axis=-1)
    return jnp.dot(codevec, quant_weight, preferred_element_type=jnp.float32).astype(jnp.bfloat16)


def remote(src, dst, send, recv, **coords):
    return pltpu.make_async_remote_copy(
        src_ref=src,
        dst_ref=dst,
        send_sem=send,
        recv_sem=recv,
        device_id=coords,
        device_id_type=pl.DeviceIdType.MESH,
    )


def greet(barrier, **coords):
    pl.semaphore_signal(
        barrier, inc=1, device_id=coords, device_id_type=pl.DeviceIdType.MESH
    )


def front_body(
    sizes,
    pairs_ref,
    cw_ref,
    pw_ref,
    embed_ref,
    mask_ref,
    taps_in,
    codes_in,
    win_ref,
    taps_ref,
    codes_ref,
    term_wide,
    term_half,
    arrived,
    feat,
    hidden,
    local_sem,
    code_send,
    code_recv,
    tap_send,
    tap_recv,
    ring_send,
    ring_recv,
    pair_send,
    pair_recv,
    sum_send,
    sum_recv,
    feat_send,
    feat_recv,
    win_send,
    win_recv,
):
    dps, seqs, tensors = sizes
    chips = seqs // 2
    dp, seq, tensor = (lax.axis_index(name) for name in ("dp", "seq", "tensor"))
    utts, frames, channels = term_wide.shape

    def other_dp(k):
        return lax.rem(dp + k, dps)

    def other_seq(k):
        return lax.rem(seq + (k + seqs) % seqs, seqs)

    def other_tensor(k):
        return lax.rem(tensor + k, tensors)

    barrier = pltpu.get_barrier_semaphore()
    for k in range(1, seqs):
        greet(barrier, seq=other_seq(k))
    for k in range(1, dps):
        for side in (-1, 0, 1):
            greet(barrier, dp=other_dp(k), seq=other_seq(side))
    for k in range(1, tensors):
        greet(barrier, tensor=other_tensor(k))
    pl.semaphore_wait(barrier, (seqs - 1) + 3 * (dps - 1) + (tensors - 1))

    pending = []

    def begin(copy):
        copy.start()
        pending.append(copy)
        return copy

    local = pltpu.make_async_copy(taps_in.at[:, dp], taps_ref.at[dp, seq], local_sem.at[0])
    local.start()
    tap_copies = [
        begin(
            remote(
                taps_in.at[:, other_dp(k)],
                taps_ref.at[dp, seq],
                tap_send.at[k - 1],
                tap_recv.at[k - 1],
                dp=other_dp(k),
            )
        )
        for k in range(1, dps)
    ]
    code_copies = [
        begin(
            remote(
                codes_in,
                codes_ref.at[seq],
                code_send.at[k - 1],
                code_recv.at[k - 1],
                seq=other_seq(k),
            )
        )
        for k in range(1, seqs)
    ]
    codes_ref[seq] = codes_in[...]

    term = jnp.dot(pairs_ref[...], cw_ref[...], preferred_element_type=jnp.float32)
    term = term.reshape(utts, frames, channels)
    term_wide[...] = term
    term_half[...] = term.astype(jnp.bfloat16)
    sum_copies = [
        begin(
            remote(
                term_half.at[other_tensor(k)],
                arrived.at[k - 1],
                sum_send.at[k - 1],
                sum_recv.at[k - 1],
                tensor=other_tensor(k),
            )
        )
        for k in range(1, tensors)
    ]

    local.wait()
    for copy in tap_copies:
        copy.wait_recv()

    core = lax.rem(seq, 2)
    sibling = seq + 1 - 2 * core

    def pass_block(slot, hop):
        block = taps_ref.at[:, lax.rem(seq + 2 * hop + seqs, seqs)]
        return begin(
            remote(block, block, pair_send.at[slot], pair_recv.at[slot], seq=sibling)
        )

    def ring(slot, hop, direction):
        block = taps_ref.at[:, lax.rem(seq + 2 * hop + seqs, seqs)]
        return begin(
            remote(
                block,
                block,
                ring_send.at[slot],
                ring_recv.at[slot],
                seq=other_seq(2 * direction),
            )
        )

    ups, downs = chips // 2, (chips - 1) // 2
    pair_copies = [pass_block(0, 0)]
    up = [ring(0, 0, 1)]
    down = [ring(ups, 0, -1)]

    def advance(step):
        if step - 1 < ups:
            up[step - 1].wait_recv()
            pair_copies.append(pass_block(step, -step))
            if step < ups:
                up.append(ring(step, -step, 1))
        if step - 1 < downs:
            down[step - 1].wait_recv()
            pair_copies.append(pass_block(ups + step, step))
            if step < downs:
                down.append(ring(ups + step, step, -1))

    summed = term_wide[tensor]
    for k, copy in enumerate(sum_copies):
        copy.wait_recv()
        summed = summed + arrived[k].astype(jnp.float32)
    row_mean = jnp.mean(summed, axis=-1, keepdims=True)
    row_square = jnp.mean(summed * summed, axis=-1, keepdims=True)
    normed = (summed - row_mean) * lax.rsqrt(row_square - row_mean * row_mean + ln_eps)
    feat[tensor] = exact_gelu(normed).astype(jnp.bfloat16)
    feat_copies = [
        begin(
            remote(
                feat.at[tensor],
                feat.at[tensor],
                feat_send.at[k - 1],
                feat_recv.at[k - 1],
                tensor=other_tensor(k),
            )
        )
        for k in range(1, tensors)
    ]
    advance(1)
    for copy in feat_copies:
        copy.wait_recv()
    features = feat[...].reshape(utts * frames, channels)
    is_masked = mask_ref[...] > 0
    for group in range(dps):
        projected = jnp.dot(features, pw_ref[group], preferred_element_type=jnp.float32)
        chosen = jnp.where(is_masked, embed_ref[group].astype(jnp.float32), projected)
        hidden[group] = chosen.astype(jnp.bfloat16).reshape(utts, frames, LANES)
    mine = pl.ds(dp * utts, utts)
    win_copies = []
    for k in range(dps):
        for side in (-1, 0, 1):
            slot = 3 * k + side + 1
            if k == 0 and side == 0:
                continue
            win_copies.append(
                begin(
                    remote(
                        hidden.at[other_dp(k)],
                        win_ref.at[mine, 1 - side],
                        win_send.at[slot],
                        win_recv.at[slot],
                        dp=other_dp(k),
                        seq=other_seq(side),
                    )
                )
            )
    win_ref[mine, 1] = hidden[dp]
    advance(2)
    for copy in win_copies:
        copy.wait_recv()

    @pl.when(seq == 0)
    def low_edge():
        win_ref[:, 0] = jnp.zeros_like(win_ref[:, 0])

    @pl.when(seq == seqs - 1)
    def high_edge():
        win_ref[:, 2] = jnp.zeros_like(win_ref[:, 2])

    for step in range(3, ups + 1):
        advance(step)
    for copy in pair_copies + code_copies:
        copy.wait_recv()
    for copy in pending:
        copy.wait_send()


def front(sizes, utts, pairs, cw, pw, embed, mask, taps, codes):
    dps, seqs, tensors = sizes
    frames = mask.shape[0] // utts
    channels = cw.shape[1]
    per, _, inner, outer = taps.shape
    vmem = pl.BlockSpec(memory_space=pltpu.VMEM)
    dma = pltpu.SemaphoreType.DMA
    hops = seqs // 2
    return pl.pallas_call(
        functools.partial(front_body, sizes),
        out_shape=(
            jax.ShapeDtypeStruct((utts * dps, 3, frames, LANES), jnp.bfloat16),
            jax.ShapeDtypeStruct((dps, seqs, per, inner, outer), jnp.bfloat16),
            jax.ShapeDtypeStruct((seqs,) + codes.shape, codes.dtype),
        ),
        in_specs=[vmem] * 7,
        out_specs=(vmem, pl.BlockSpec(memory_space=pl.ANY), vmem),
        scratch_shapes=[
            pltpu.VMEM((utts, frames, channels), jnp.float32),
            pltpu.VMEM((utts, frames, channels), jnp.bfloat16),
            pltpu.VMEM((tensors - 1, frames, channels), jnp.bfloat16),
            pltpu.VMEM((utts, frames, channels), jnp.bfloat16),
            pltpu.VMEM((dps, utts, frames, LANES), jnp.bfloat16),
            dma((1,)),
            dma((seqs - 1,)),
            dma((seqs - 1,)),
            dma((dps - 1,)),
            dma((dps - 1,)),
            dma((hops - 1,)),
            dma((hops - 1,)),
            dma((hops,)),
            dma((hops,)),
            dma((tensors - 1,)),
            dma((tensors - 1,)),
            dma((tensors - 1,)),
            dma((tensors - 1,)),
            dma((3 * dps,)),
            dma((3 * dps,)),
        ],
        compiler_params=pltpu.CompilerParams(
            collective_id=0, has_side_effects=True, vmem_limit_bytes=40 * 2**20
        ),
    )(pairs, cw, pw, embed, mask, taps, codes)


def conv_body(x_ref, w_ref, o_ref, xf, xc, wc, acc):
    step = pl.program_id(0)
    utts, rows, _ = x_ref.shape
    inner, outer = w_ref.shape[1:]
    frames = rows - KERNEL
    span = frames + SHIFTS
    kept = rows - SHIFTS
    joint = 4

    @pl.when(step == 0)
    def shift_copies():
        wc[...] = jnp.zeros_like(wc)
        acc[...] = jnp.zeros_like(acc)

        @pl.loop(0, utts)
        def one(u):
            xf[...] = x_ref[u].astype(jnp.float32)
            for j in range(SHIFTS):
                xc[u, :, j * LANES : (j + 1) * LANES] = xf[j : j + kept, :].astype(jnp.bfloat16)

    for half in range(2):
        for j in range(SHIFTS):
            wc[
                j * LANES : j * LANES + inner, half * LANES : half * LANES + outer
            ] = w_ref[half * SHIFTS + j]
    first = pl.multiple_of(step * (2 * SHIFTS), 2 * SHIFTS)

    @pl.loop(0, utts // joint)
    def multiply(chunk):
        here = pl.ds(chunk * joint, joint)
        window = xc[here, pl.ds(first, span), :].reshape(joint * span, SHIFTS * LANES)
        acc[here] += jnp.dot(window, wc[...], preferred_element_type=jnp.float32).reshape(
            joint, span, 2 * LANES
        )

    @pl.when(step == pl.num_programs(0) - 1)
    def finish():
        @pl.loop(0, utts)
        def one(u):
            conv_out = acc[u, :frames, :LANES] + acc[u, SHIFTS:, LANES:]
            own = x_ref[u, KERNEL // 2 : KERNEL // 2 + frames, :].astype(jnp.float32)
            o_ref[u] = (own + exact_gelu(conv_out)).astype(jnp.bfloat16)


def grouped_conv(windows, taps):
    utts, rows, _ = windows.shape
    count, inner, outer = taps.shape
    frames = rows - KERNEL
    span = frames + SHIFTS
    steps = count // (2 * SHIFTS)
    return pl.pallas_call(
        conv_body,
        grid=(steps,),
        out_shape=jax.ShapeDtypeStruct((utts, frames, LANES), jnp.bfloat16),
        in_specs=[
            pl.BlockSpec((utts, rows, LANES), lambda p: (0, 0, 0)),
            pl.BlockSpec((2 * SHIFTS, inner, outer), lambda p: (p, 0, 0)),
        ],
        out_specs=pl.BlockSpec((utts, frames, LANES), lambda p: (0, 0, 0)),
        scratch_shapes=[
            pltpu.VMEM((rows, LANES), jnp.float32),
            pltpu.VMEM((utts, rows - SHIFTS, SHIFTS * LANES), jnp.bfloat16),
            pltpu.VMEM((SHIFTS * LANES, 2 * LANES), jnp.bfloat16),
            pltpu.VMEM((utts, span, 2 * LANES), jnp.float32),
        ],
        compiler_params=pltpu.CompilerParams(vmem_limit_bytes=48 * 2**20),
    )(windows, taps)


def back_body(
    sizes,
    mixed_ref,
    fw_ref,
    t_ref,
    own_ref,
    tn_ref,
    count_ref,
    mask_ref,
    o_ref,
    gathered,
    part_wide,
    part_half,
    arrived,
    mix_send,
    mix_recv,
    sum_send,
    sum_recv,
):
    dps, _, tensors = sizes
    dp, tensor = lax.axis_index("dp"), lax.axis_index("tensor")
    utts, frames, code_dim = part_wide.shape
    inner = fw_ref.shape[1]

    barrier = pltpu.get_barrier_semaphore()
    for k in range(1, dps):
        greet(barrier, dp=lax.rem(dp + k, dps))
    for k in range(1, tensors):
        greet(barrier, tensor=lax.rem(tensor + k, tensors))
    pl.semaphore_wait(barrier, dps - 1 + tensors - 1)

    mix_copies = []
    for k in range(1, dps):
        there = lax.rem(dp + k, dps)
        copy = remote(
            mixed_ref.at[pl.ds(there * utts, utts)],
            gathered.at[dp],
            mix_send.at[k - 1],
            mix_recv.at[k - 1],
            dp=there,
        )
        copy.start()
        mix_copies.append(copy)
    gathered[dp] = mixed_ref[pl.ds(dp * utts, utts)]
    for copy in mix_copies:
        copy.wait_recv()
    sum_copies = []
    for k in range(tensors):
        there = lax.rem(tensor + k + 1, tensors)
        total = jnp.zeros((frames, code_dim), jnp.float32)
        for group in range(dps):
            rows = gathered[group, there][:, :inner]
            total += jnp.dot(rows, fw_ref[group], preferred_element_type=jnp.float32)
        if k < tensors - 1:
            part_half[k] = total.astype(jnp.bfloat16)
            copy = remote(
                part_half.at[k],
                arrived.at[k],
                sum_send.at[k],
                sum_recv.at[k],
                tensor=there,
            )
            copy.start()
            sum_copies.append(copy)
    for k, copy in enumerate(sum_copies):
        copy.wait_recv()
        total += arrived[k].astype(jnp.float32)
    context = total.astype(jnp.bfloat16)
    scores = lax.dot_general(
        context, t_ref[...], (((1,), (1,)), ((), ())), preferred_element_type=jnp.float32
    )
    wide = context.astype(jnp.float32)
    own = own_ref[...].astype(jnp.float32)
    ctx_norm = jnp.sum(wide * wide, axis=-1, keepdims=True) + norm_eps
    own_norm = jnp.sum(own * own, axis=-1, keepdims=True) + norm_eps
    pos_dot = jnp.sum(wide * own, axis=-1, keepdims=True)
    positive = pos_dot * lax.rsqrt(ctx_norm * own_norm) / logit_temp
    logits = scores * lax.rsqrt(ctx_norm * (tn_ref[...] + norm_eps)) / logit_temp
    negatives = jnp.sum(count_ref[...] * jnp.exp(logits), axis=-1, keepdims=True)
    loss = jnp.log(jnp.exp(positive) + negatives) - positive
    o_ref[...] = jnp.where(mask_ref[...] > 0, loss, 0.0)
    for copy in mix_copies + sum_copies:
        copy.wait_send()


def back(sizes, mixed, fw, targets, own, norms, counts, mask):
    dps, _, tensors = sizes
    utts, frames = mixed.shape[0] // dps, mixed.shape[1]
    code_dim = fw.shape[-1]
    dma = pltpu.SemaphoreType.DMA
    return pl.pallas_call(
        functools.partial(back_body, sizes),
        out_shape=jax.ShapeDtypeStruct((frames, 1), jnp.float32),
        in_specs=[pl.BlockSpec(memory_space=pltpu.VMEM)] * 7,
        out_specs=pl.BlockSpec(memory_space=pltpu.VMEM),
        scratch_shapes=[
            pltpu.VMEM((dps, utts, frames, LANES), jnp.bfloat16),
            pltpu.VMEM((utts, frames, code_dim), jnp.float32),
            pltpu.VMEM((tensors - 1, frames, code_dim), jnp.bfloat16),
            pltpu.VMEM((tensors - 1, frames, code_dim), jnp.bfloat16),
            dma((dps - 1,)),
            dma((dps - 1,)),
            dma((tensors - 1,)),
            dma((tensors - 1,)),
        ],
        compiler_params=pltpu.CompilerParams(
            collective_id=1, has_side_effects=True, vmem_limit_bytes=32 * 2**20
        ),
    )(mixed, fw, targets, own, norms, counts, mask)


def on_device(
    feature_in,
    conv_weight,
    proj_weight,
    mask_embed,
    pos_weight,
    final_weight,
    codebook,
    quant_weight,
    mask_starts,
    code_choice,
    negative_ids,
):
    utts, sample_rows, channels = feature_in.shape
    frames = sample_rows // 2
    sizes = tuple(lax.axis_size(name) for name in ("dp", "seq", "tensor"))
    dps, seqs, tensors = sizes
    groups, inner = pos_weight.shape[1], pos_weight.shape[2]
    padding = LANES - inner

    pairs = feature_in.reshape(utts * frames, 2 * channels)
    cw = conv_weight.reshape(2 * channels, conv_weight.shape[2])
    pw = proj_weight.reshape(proj_weight.shape[0], groups, inner).transpose(1, 0, 2)
    pw = jnp.pad(pw, ((0, 0), (0, 0), (0, padding)))
    embed = jnp.pad(mask_embed.reshape(groups, 1, inner), ((0, 0), (0, 0), (0, padding)))
    positions = (lax.axis_index("seq") * frames + jnp.arange(frames, dtype=jnp.int32))[
        None, :, None
    ]
    starts = mask_starts[:, None, :]
    masked = jnp.any((positions >= starts) & (positions < starts + MASK_LEN), axis=-1)
    masked = masked.astype(jnp.float32).reshape(utts * frames, 1)

    windows, taps, codes = front(
        sizes,
        utts,
        pairs,
        cw,
        pw,
        embed,
        masked,
        pos_weight,
        code_choice.reshape(1, -1),
    )
    mixed = grouped_conv(
        windows.reshape(dps * utts, 3 * frames, LANES), taps.reshape(-1, inner, inner)
    )

    all_codes = codes.reshape(seqs * frames, code_choice.shape[-1])
    all_targets = make_targets(all_codes, codebook, quant_weight)
    wide_targets = all_targets.astype(jnp.float32)
    tgt_norm = jnp.sum(wide_targets * wide_targets, axis=-1)[None, :]
    own_targets = lax.dynamic_slice_in_dim(
        all_targets, lax.axis_index("seq") * frames, frames, 0
    )
    ids = negative_ids.reshape(frames, negative_ids.shape[-1])
    frame_row = jnp.arange(seqs * frames, dtype=jnp.int32)
    counts = jnp.sum((ids[:, :, None] == frame_row).astype(jnp.float32), axis=1)
    own_masked = lax.dynamic_slice_in_dim(
        masked, lax.axis_index("tensor") * frames, frames, 0
    )
    loss = back(
        sizes,
        mixed,
        final_weight.reshape(groups, inner, final_weight.shape[1]),
        all_targets,
        own_targets,
        tgt_norm,
        counts,
        own_masked,
    )
    return loss.reshape(1, frames)


def solution(mesh):
    return jax.shard_map(
        on_device,
        mesh=mesh,
        in_specs=(
            P("dp", "seq", "tensor"),
            P(None, "tensor", None),
            P(None, "tensor"),
            P("tensor"),
            P(("dp", "seq"), "tensor", None, None),
            P("tensor", None),
            P(),
            P(),
            P("dp", None),
            P(("dp", "tensor"), "seq", None),
            P(("dp", "tensor"), "seq", None),
        ),
        out_specs=P(("dp", "tensor"), "seq"),
        check_vma=False,
    )
```

```python
import functools

import jax
import jax.numpy as jnp
from jax import lax
from jax.experimental import pallas as pl
from jax.experimental.pallas import tpu as pltpu
from jax.sharding import PartitionSpec as P

KERNEL = 128
MASK_LEN = 10
SHIFTS = 16
LANES = 128


ln_eps = 1e-05
norm_eps = 1e-06
logit_temp = 0.1


def exact_gelu(value):
    return 0.5 * value * (1.0 + lax.erf(value * (0.5**0.5)))


def remote(src, dst, send, recv, **coords):
    return pltpu.make_async_remote_copy(
        src_ref=src,
        dst_ref=dst,
        send_sem=send,
        recv_sem=recv,
        device_id=coords,
        device_id_type=pl.DeviceIdType.MESH,
    )


def greet(barrier, **coords):
    pl.semaphore_signal(
        barrier, inc=1, device_id=coords, device_id_type=pl.DeviceIdType.MESH
    )


def front_body(
    sizes,
    pairs_ref,
    cw_ref,
    pw_ref,
    embed_ref,
    mask_ref,
    taps_in,
    codes_in,
    book_ref,
    qw_ref,
    win_ref,
    taps_ref,
    targets_ref,
    norms_ref,
    codes_ref,
    choice,
    codevec,
    term_wide,
    term_half,
    arrived,
    feat,
    hidden,
    local_sem,
    code_send,
    code_recv,
    tap_send,
    tap_recv,
    ring_send,
    ring_recv,
    pair_send,
    pair_recv,
    sum_send,
    sum_recv,
    feat_send,
    feat_recv,
    win_send,
    win_recv,
):
    dps, seqs, tensors = sizes
    chips = seqs // 2
    dp, seq, tensor = (lax.axis_index(name) for name in ("dp", "seq", "tensor"))
    utts, frames, channels = term_wide.shape

    def other_dp(k):
        return lax.rem(dp + k, dps)

    def other_seq(k):
        return lax.rem(seq + (k + seqs) % seqs, seqs)

    def other_tensor(k):
        return lax.rem(tensor + k, tensors)

    barrier = pltpu.get_barrier_semaphore()
    for k in range(1, seqs):
        greet(barrier, seq=other_seq(k))
    for k in range(1, dps):
        for side in (-1, 0, 1):
            greet(barrier, dp=other_dp(k), seq=other_seq(side))
    for k in range(1, tensors):
        greet(barrier, tensor=other_tensor(k))
    pl.semaphore_wait(barrier, (seqs - 1) + 3 * (dps - 1) + (tensors - 1))

    pending = []

    def begin(copy):
        copy.start()
        pending.append(copy)
        return copy

    local = pltpu.make_async_copy(taps_in.at[:, dp], taps_ref.at[dp, seq], local_sem.at[0])
    local.start()
    tap_copies = [
        begin(
            remote(
                taps_in.at[:, other_dp(k)],
                taps_ref.at[dp, seq],
                tap_send.at[k - 1],
                tap_recv.at[k - 1],
                dp=other_dp(k),
            )
        )
        for k in range(1, dps)
    ]
    code_copies = [
        begin(
            remote(
                codes_in,
                codes_ref.at[seq],
                code_send.at[k - 1],
                code_recv.at[k - 1],
                seq=other_seq(k),
            )
        )
        for k in range(1, seqs)
    ]
    codes_ref[seq] = codes_in[...]

    term = jnp.dot(pairs_ref[...], cw_ref[...], preferred_element_type=jnp.float32)
    term = term.reshape(utts, frames, channels)
    term_wide[...] = term
    term_half[...] = term.astype(jnp.bfloat16)
    sum_copies = [
        begin(
            remote(
                term_half.at[other_tensor(k)],
                arrived.at[k - 1],
                sum_send.at[k - 1],
                sum_recv.at[k - 1],
                tensor=other_tensor(k),
            )
        )
        for k in range(1, tensors)
    ]

    local.wait()
    for copy in tap_copies:
        copy.wait_recv()

    core = lax.rem(seq, 2)
    sibling = seq + 1 - 2 * core

    def pass_block(slot, hop):
        block = taps_ref.at[:, lax.rem(seq + 2 * hop + seqs, seqs)]
        return begin(
            remote(block, block, pair_send.at[slot], pair_recv.at[slot], seq=sibling)
        )

    def ring(slot, hop, direction):
        block = taps_ref.at[:, lax.rem(seq + 2 * hop + seqs, seqs)]
        return begin(
            remote(
                block,
                block,
                ring_send.at[slot],
                ring_recv.at[slot],
                seq=other_seq(2 * direction),
            )
        )

    ups, downs = chips // 2, (chips - 1) // 2
    pair_copies = [pass_block(0, 0)]
    up = [ring(0, 0, 1)]
    down = [ring(ups, 0, -1)]

    def advance(step):
        if step - 1 < ups:
            up[step - 1].wait_recv()
            pair_copies.append(pass_block(step, -step))
            if step < ups:
                up.append(ring(step, -step, 1))
        if step - 1 < downs:
            down[step - 1].wait_recv()
            pair_copies.append(pass_block(ups + step, step))
            if step < downs:
                down.append(ring(ups + step, step, -1))

    summed = term_wide[tensor]
    for k, copy in enumerate(sum_copies):
        copy.wait_recv()
        summed = summed + arrived[k].astype(jnp.float32)
    row_mean = jnp.mean(summed, axis=-1, keepdims=True)
    row_square = jnp.mean(summed * summed, axis=-1, keepdims=True)
    normed = (summed - row_mean) * lax.rsqrt(row_square - row_mean * row_mean + ln_eps)
    feat[tensor] = exact_gelu(normed).astype(jnp.bfloat16)
    feat_copies = [
        begin(
            remote(
                feat.at[tensor],
                feat.at[tensor],
                feat_send.at[k - 1],
                feat_recv.at[k - 1],
                tensor=other_tensor(k),
            )
        )
        for k in range(1, tensors)
    ]
    advance(1)
    for copy in feat_copies:
        copy.wait_recv()
    features = feat[...].reshape(utts * frames, channels)
    is_masked = mask_ref[...] > 0
    inner = embed_ref.shape[-1]
    hidden[...] = jnp.zeros_like(hidden)
    for group in range(dps):
        projected = lax.dot_general(
            features,
            pw_ref[group * inner : (group + 1) * inner, :],
            (((1,), (1,)), ((), ())),
            preferred_element_type=jnp.float32,
        )
        chosen = jnp.where(is_masked, embed_ref[group].astype(jnp.float32), projected)
        hidden[group, :, :, :inner] = chosen.astype(jnp.bfloat16).reshape(utts, frames, inner)
    mine = pl.ds(dp * utts, utts)
    win_copies = []
    for k in range(dps):
        for side in (-1, 0, 1):
            slot = 3 * k + side + 1
            if k == 0 and side == 0:
                continue
            win_copies.append(
                begin(
                    remote(
                        hidden.at[other_dp(k)],
                        win_ref.at[mine, 1 - side],
                        win_send.at[slot],
                        win_recv.at[slot],
                        dp=other_dp(k),
                        seq=other_seq(side),
                    )
                )
            )
    win_ref[mine, 1] = hidden[dp]
    for copy in code_copies:
        copy.wait_recv()
    for block in range(seqs):
        choice[:, block * frames : (block + 1) * frames] = codes_ref[block]
    entries, width = book_ref.shape[1:]
    half = choice.shape[1] // 2

    def make_targets(part):
        here = slice(part * half, (part + 1) * half)
        for qgroup in range(book_ref.shape[0]):
            row = lax.broadcasted_iota(jnp.int32, (entries, half), 0)
            onehot = jnp.where(row == choice[qgroup : qgroup + 1, here], 1.0, 0.0)
            codevec[:, qgroup * width : (qgroup + 1) * width] = lax.dot_general(
                onehot.astype(jnp.bfloat16),
                book_ref[qgroup],
                (((0,), (0,)), ((), ())),
                preferred_element_type=jnp.float32,
            ).astype(jnp.bfloat16)
        made = jnp.dot(codevec[...], qw_ref[...], preferred_element_type=jnp.float32)
        made = made.astype(jnp.bfloat16)
        targets_ref[here, :] = made
        made = made.astype(jnp.float32)
        norm = jnp.sum(made * made, axis=-1, keepdims=True)
        norms_ref[:, here] = jnp.transpose(jnp.broadcast_to(norm, (half, LANES)))[:1]

    make_targets(0)
    advance(2)
    make_targets(1)
    for copy in win_copies:
        copy.wait_recv()

    @pl.when(seq == 0)
    def low_edge():
        win_ref[:, 0] = jnp.zeros_like(win_ref[:, 0])

    @pl.when(seq == seqs - 1)
    def high_edge():
        win_ref[:, 2] = jnp.zeros_like(win_ref[:, 2])

    for step in range(3, ups + 1):
        advance(step)
    for copy in pair_copies:
        copy.wait_recv()
    for copy in pending:
        copy.wait_send()


def front(sizes, utts, pairs, cw, pw, embed, mask, taps, codes, book, qw):
    dps, seqs, tensors = sizes
    frames = mask.shape[0] // utts
    channels = cw.shape[1]
    per, _, inner, outer = taps.shape
    vmem = pl.BlockSpec(memory_space=pltpu.VMEM)
    dma = pltpu.SemaphoreType.DMA
    hops = seqs // 2
    return pl.pallas_call(
        functools.partial(front_body, sizes),
        out_shape=(
            jax.ShapeDtypeStruct((utts * dps, 3, frames, LANES), jnp.bfloat16),
            jax.ShapeDtypeStruct((dps, seqs, per, inner, outer), jnp.bfloat16),
            jax.ShapeDtypeStruct((seqs * frames, qw.shape[1]), jnp.bfloat16),
            jax.ShapeDtypeStruct((1, seqs * frames), jnp.float32),
        ),
        in_specs=[vmem] * 9,
        out_specs=(vmem, pl.BlockSpec(memory_space=pl.ANY), vmem, vmem),
        scratch_shapes=[
            pltpu.VMEM((seqs,) + codes.shape, codes.dtype),
            pltpu.VMEM((codes.shape[0], seqs * frames), codes.dtype),
            pltpu.VMEM((seqs * frames // 2, qw.shape[0]), jnp.bfloat16),
            pltpu.VMEM((utts, frames, channels), jnp.float32),
            pltpu.VMEM((utts, frames, channels), jnp.bfloat16),
            pltpu.VMEM((tensors - 1, frames, channels), jnp.bfloat16),
            pltpu.VMEM((utts, frames, channels), jnp.bfloat16),
            pltpu.VMEM((dps, utts, frames, LANES), jnp.bfloat16),
            dma((1,)),
            dma((seqs - 1,)),
            dma((seqs - 1,)),
            dma((dps - 1,)),
            dma((dps - 1,)),
            dma((hops - 1,)),
            dma((hops - 1,)),
            dma((hops,)),
            dma((hops,)),
            dma((tensors - 1,)),
            dma((tensors - 1,)),
            dma((tensors - 1,)),
            dma((tensors - 1,)),
            dma((3 * dps,)),
            dma((3 * dps,)),
        ],
        compiler_params=pltpu.CompilerParams(
            collective_id=0, has_side_effects=True, vmem_limit_bytes=40 * 2**20
        ),
    )(pairs, cw, pw, embed, mask, taps, codes, book, qw)


def conv_body(x_ref, w_ref, o_ref, xf, xc, wc, acc):
    step = pl.program_id(0)
    utts, rows, _ = x_ref.shape
    inner, outer = w_ref.shape[1:]
    frames = rows - KERNEL
    span = frames + SHIFTS
    kept = rows - SHIFTS
    joint = 4

    @pl.when(step == 0)
    def shift_copies():
        wc[...] = jnp.zeros_like(wc)
        acc[...] = jnp.zeros_like(acc)

        @pl.loop(0, utts)
        def one(u):
            xf[...] = x_ref[u].astype(jnp.float32)
            for j in range(SHIFTS):
                xc[u, :, j * LANES : (j + 1) * LANES] = xf[j : j + kept, :].astype(jnp.bfloat16)

    for half in range(2):
        for j in range(SHIFTS):
            wc[
                j * LANES : j * LANES + inner, half * LANES : half * LANES + outer
            ] = w_ref[half * SHIFTS + j]
    first = pl.multiple_of(step * (2 * SHIFTS), 2 * SHIFTS)

    @pl.loop(0, utts // joint)
    def multiply(chunk):
        here = pl.ds(chunk * joint, joint)
        window = xc[here, pl.ds(first, span), :].reshape(joint * span, SHIFTS * LANES)
        acc[here] += jnp.dot(window, wc[...], preferred_element_type=jnp.float32).reshape(
            joint, span, 2 * LANES
        )

    @pl.when(step == pl.num_programs(0) - 1)
    def finish():
        @pl.loop(0, utts)
        def one(u):
            conv_out = acc[u, :frames, :LANES] + acc[u, SHIFTS:, LANES:]
            own = x_ref[u, KERNEL // 2 : KERNEL // 2 + frames, :].astype(jnp.float32)
            o_ref[u] = (own + exact_gelu(conv_out)).astype(jnp.bfloat16)


def grouped_conv(windows, taps):
    utts, rows, _ = windows.shape
    count, inner, outer = taps.shape
    frames = rows - KERNEL
    span = frames + SHIFTS
    steps = count // (2 * SHIFTS)
    return pl.pallas_call(
        conv_body,
        grid=(steps,),
        out_shape=jax.ShapeDtypeStruct((utts, frames, LANES), jnp.bfloat16),
        in_specs=[
            pl.BlockSpec((utts, rows, LANES), lambda p: (0, 0, 0)),
            pl.BlockSpec((2 * SHIFTS, inner, outer), lambda p: (p, 0, 0)),
        ],
        out_specs=pl.BlockSpec((utts, frames, LANES), lambda p: (0, 0, 0)),
        scratch_shapes=[
            pltpu.VMEM((rows, LANES), jnp.float32),
            pltpu.VMEM((utts, rows - SHIFTS, SHIFTS * LANES), jnp.bfloat16),
            pltpu.VMEM((SHIFTS * LANES, 2 * LANES), jnp.bfloat16),
            pltpu.VMEM((utts, span, 2 * LANES), jnp.float32),
        ],
        compiler_params=pltpu.CompilerParams(vmem_limit_bytes=48 * 2**20),
    )(windows, taps)


def back_body(
    sizes,
    mixed_ref,
    fw_ref,
    o_ref,
    gathered,
    part_half,
    arrived,
    mix_send,
    mix_recv,
    sum_send,
    sum_recv,
):
    dps, _, tensors = sizes
    dp, tensor = lax.axis_index("dp"), lax.axis_index("tensor")
    _, utts, frames, _ = gathered.shape
    code_dim = o_ref.shape[1]
    inner = fw_ref.shape[1]

    barrier = pltpu.get_barrier_semaphore()
    for k in range(1, dps):
        greet(barrier, dp=lax.rem(dp + k, dps))
    for k in range(1, tensors):
        greet(barrier, tensor=lax.rem(tensor + k, tensors))
    pl.semaphore_wait(barrier, dps - 1 + tensors - 1)

    mix_copies = []
    for k in range(1, dps):
        there = lax.rem(dp + k, dps)
        copy = remote(
            mixed_ref.at[pl.ds(there * utts, utts)],
            gathered.at[dp],
            mix_send.at[k - 1],
            mix_recv.at[k - 1],
            dp=there,
        )
        copy.start()
        mix_copies.append(copy)
    gathered[dp] = mixed_ref[pl.ds(dp * utts, utts)]
    for copy in mix_copies:
        copy.wait_recv()
    sum_copies = []
    for k in range(tensors):
        there = lax.rem(tensor + k + 1, tensors)
        total = jnp.zeros((frames, code_dim), jnp.float32)
        for group in range(dps):
            rows = gathered[group, there][:, :inner]
            total += jnp.dot(rows, fw_ref[group], preferred_element_type=jnp.float32)
        if k < tensors - 1:
            part_half[k] = total.astype(jnp.bfloat16)
            copy = remote(
                part_half.at[k],
                arrived.at[k],
                sum_send.at[k],
                sum_recv.at[k],
                tensor=there,
            )
            copy.start()
            sum_copies.append(copy)
    for k, copy in enumerate(sum_copies):
        copy.wait_recv()
        total += arrived[k].astype(jnp.float32)
    o_ref[...] = total.astype(jnp.bfloat16)
    for copy in mix_copies + sum_copies:
        copy.wait_send()


def back(sizes, mixed, fw):
    dps, _, tensors = sizes
    utts, frames = mixed.shape[0] // dps, mixed.shape[1]
    code_dim = fw.shape[-1]
    dma = pltpu.SemaphoreType.DMA
    return pl.pallas_call(
        functools.partial(back_body, sizes),
        out_shape=jax.ShapeDtypeStruct((frames, code_dim), jnp.bfloat16),
        in_specs=[pl.BlockSpec(memory_space=pltpu.VMEM)] * 2,
        out_specs=pl.BlockSpec(memory_space=pltpu.VMEM),
        scratch_shapes=[
            pltpu.VMEM((dps, utts, frames, LANES), jnp.bfloat16),
            pltpu.VMEM((tensors - 1, frames, code_dim), jnp.bfloat16),
            pltpu.VMEM((tensors - 1, frames, code_dim), jnp.bfloat16),
            dma((dps - 1,)),
            dma((dps - 1,)),
            dma((tensors - 1,)),
            dma((tensors - 1,)),
        ],
        compiler_params=pltpu.CompilerParams(
            collective_id=1, has_side_effects=True, vmem_limit_bytes=32 * 2**20
        ),
    )(mixed, fw)


def loss_body(c_ref, t_ref, tn_ref, ids_ref, mask_ref, o_ref, ids):
    context = c_ref[...]
    frames, negs = ids_ref.shape
    ids[...] = jnp.zeros_like(ids)
    ids[:, :negs] = ids_ref[...]
    first = pl.multiple_of(lax.axis_index("seq") * frames, frames)
    scores = lax.dot_general(
        context, t_ref[...], (((1,), (1,)), ((), ())), preferred_element_type=jnp.float32
    )
    wide = context.astype(jnp.float32)
    own = t_ref[pl.ds(first, frames), :].astype(jnp.float32)
    ctx_norm = jnp.sum(wide * wide, axis=-1, keepdims=True) + norm_eps
    own_norm = jnp.sum(own * own, axis=-1, keepdims=True) + norm_eps
    pos_dot = jnp.sum(wide * own, axis=-1, keepdims=True)
    positive = pos_dot * lax.rsqrt(ctx_norm * own_norm) / logit_temp
    logits = scores * lax.rsqrt(ctx_norm * (tn_ref[...] + norm_eps)) / logit_temp
    powers = jnp.exp(logits)
    chosen = ids[...]
    lane = chosen % LANES
    chunk = chosen // LANES
    picked = jnp.zeros((frames, LANES), jnp.float32)
    for c in range(powers.shape[1] // LANES):
        found = jnp.take_along_axis(
            powers[:, c * LANES : (c + 1) * LANES], lane, axis=1, mode="promise_in_bounds"
        )
        picked = jnp.where(chunk == c, found, picked)
    real = lax.broadcasted_iota(jnp.int32, picked.shape, 1) < negs
    negatives = jnp.sum(jnp.where(real, picked, 0.0), axis=-1, keepdims=True)
    loss = jnp.log(jnp.exp(positive) + negatives) - positive
    o_ref[...] = jnp.where(mask_ref[...] > 0, loss, 0.0)


def losses(context, targets, norms, ids, mask):
    return pl.pallas_call(
        loss_body,
        out_shape=jax.ShapeDtypeStruct((ids.shape[0], 1), jnp.float32),
        scratch_shapes=[pltpu.VMEM((ids.shape[0], LANES), jnp.int32)],
        compiler_params=pltpu.CompilerParams(vmem_limit_bytes=24 * 2**20),
    )(context, targets, norms, ids, mask)


def on_device(
    feature_in,
    conv_weight,
    proj_weight,
    mask_embed,
    pos_weight,
    final_weight,
    codebook,
    quant_weight,
    mask_starts,
    code_choice,
    negative_ids,
):
    utts, sample_rows, channels = feature_in.shape
    frames = sample_rows // 2
    sizes = tuple(lax.axis_size(name) for name in ("dp", "seq", "tensor"))
    dps, seqs, tensors = sizes
    groups, inner = pos_weight.shape[1], pos_weight.shape[2]

    pairs = feature_in.reshape(utts * frames, 2 * channels)
    cw = conv_weight.reshape(2 * channels, conv_weight.shape[2])
    embed = mask_embed.reshape(groups, 1, inner)
    positions = (lax.axis_index("seq") * frames + jnp.arange(frames, dtype=jnp.int32))[
        None, :, None
    ]
    starts = mask_starts[:, None, :]
    masked = jnp.any((positions >= starts) & (positions < starts + MASK_LEN), axis=-1)
    masked = masked.astype(jnp.float32).reshape(utts * frames, 1)

    windows, taps, targets, norms = front(
        sizes,
        utts,
        pairs,
        cw,
        proj_weight.T,
        embed,
        masked,
        pos_weight,
        code_choice[0].T,
        codebook,
        quant_weight,
    )
    mixed = grouped_conv(
        windows.reshape(dps * utts, 3 * frames, LANES), taps.reshape(-1, inner, inner)
    )
    context = back(sizes, mixed, final_weight.reshape(groups, inner, final_weight.shape[1]))
    own_masked = lax.dynamic_slice_in_dim(
        masked, lax.axis_index("tensor") * frames, frames, 0
    )
    loss = losses(context, targets, norms, negative_ids[0], own_masked)
    return loss.reshape(1, frames)


def solution(mesh):
    return jax.shard_map(
        on_device,
        mesh=mesh,
        in_specs=(
            P("dp", "seq", "tensor"),
            P(None, "tensor", None),
            P(None, "tensor"),
            P("tensor"),
            P(("dp", "seq"), "tensor", None, None),
            P("tensor", None),
            P(),
            P(),
            P("dp", None),
            P(("dp", "tensor"), "seq", None),
            P(("dp", "tensor"), "seq", None),
        ),
        out_specs=P(("dp", "tensor"), "seq"),
        check_vma=False,
    )
```

```python
import functools

import jax
import jax.numpy as jnp
from jax import lax
from jax.experimental import pallas as pl
from jax.experimental.pallas import tpu as pltpu
from jax.sharding import PartitionSpec as P

KERNEL = 128
MASK_LEN = 10
SHIFTS = 16
LANES = 128


ln_eps = 1e-05
norm_eps = 1e-06
logit_temp = 0.1


def exact_gelu(value):
    return 0.5 * value * (1.0 + lax.erf(value * (0.5**0.5)))


def remote(src, dst, send, recv, **coords):
    return pltpu.make_async_remote_copy(
        src_ref=src,
        dst_ref=dst,
        send_sem=send,
        recv_sem=recv,
        device_id=coords,
        device_id_type=pl.DeviceIdType.MESH,
    )


def greet(barrier, **coords):
    pl.semaphore_signal(
        barrier, inc=1, device_id=coords, device_id_type=pl.DeviceIdType.MESH
    )


def frame_mask(starts, first, frames):
    position = first + lax.broadcasted_iota(jnp.int32, (frames, starts.shape[1]), 0)
    inside = (position >= starts) & (position < starts + MASK_LEN)
    return jnp.max(jnp.where(inside, 1.0, 0.0), axis=-1, keepdims=True)


def main_body(
    sizes,
    x_hbm,
    cw_hbm,
    pw_hbm,
    embed_hbm,
    starts_hbm,
    book_hbm,
    qw_hbm,
    fw_hbm,
    taps_in,
    codes_in,
    context_ref,
    targets_ref,
    norms_ref,
    x_in,
    cw_ref,
    pw_ref,
    embed_ref,
    starts_ref,
    book_ref,
    qw_ref,
    fw_ref,
    taps_ref,
    codes_ref,
    choice,
    codevec,
    x_wide,
    term_wide,
    term_half,
    arrived,
    feat,
    hidden,
    win_ref,
    xf,
    xc,
    wc,
    acc,
    mixed,
    gathered,
    part_half,
    part_arrived,
    load_sem,
    local_sem,
    code_send,
    code_recv,
    tap_send,
    tap_recv,
    ring_send,
    ring_recv,
    pair_send,
    pair_recv,
    sum_send,
    sum_recv,
    feat_send,
    feat_recv,
    win_send,
    win_recv,
    mix_send,
    mix_recv,
    part_send,
    part_recv,
):
    dps, seqs, tensors = sizes
    chips = seqs // 2
    dp, seq, tensor = (lax.axis_index(name) for name in ("dp", "seq", "tensor"))
    utts, frames, channels = term_wide.shape
    inner = taps_ref.shape[-1]

    def other_dp(k):
        return lax.rem(dp + k, dps)

    def other_seq(k):
        return lax.rem(seq + (k + seqs) % seqs, seqs)

    def other_tensor(k):
        return lax.rem(tensor + k, tensors)

    loads = [
        pltpu.make_async_copy(source, target, load_sem.at[index])
        for index, (source, target) in enumerate(
            (
                (x_hbm, x_in),
                (cw_hbm, cw_ref),
                (pw_hbm, pw_ref),
                (embed_hbm, embed_ref),
                (starts_hbm, starts_ref),
                (book_hbm, book_ref),
                (qw_hbm, qw_ref),
                (fw_hbm, fw_ref),
            )
        )
    ]
    for copy in loads:
        copy.start()
    local = pltpu.make_async_copy(taps_in.at[:, dp], taps_ref.at[dp, seq], local_sem.at[0])
    local.start()
    local_codes = pltpu.make_async_copy(codes_in, codes_ref.at[seq], local_sem.at[1])
    local_codes.start()

    barrier = pltpu.get_barrier_semaphore()
    for k in range(1, seqs):
        greet(barrier, seq=other_seq(k))
    for k in range(1, dps):
        for side in (-1, 0, 1):
            greet(barrier, dp=other_dp(k), seq=other_seq(side))
    for k in range(1, tensors):
        greet(barrier, tensor=other_tensor(k))
    pl.semaphore_wait(barrier, (seqs - 1) + 3 * (dps - 1) + (tensors - 1))

    pending = []

    def begin(copy):
        copy.start()
        pending.append(copy)
        return copy

    tap_copies = [
        begin(
            remote(
                taps_in.at[:, other_dp(k)],
                taps_ref.at[dp, seq],
                tap_send.at[k - 1],
                tap_recv.at[k - 1],
                dp=other_dp(k),
            )
        )
        for k in range(1, dps)
    ]
    code_copies = [
        begin(
            remote(
                codes_in,
                codes_ref.at[seq],
                code_send.at[k - 1],
                code_recv.at[k - 1],
                seq=other_seq(k),
            )
        )
        for k in range(1, seqs)
    ]

    loads[0].wait()
    loads[1].wait()
    x_wide[...] = x_in[...].reshape(x_wide.shape).astype(jnp.float32)
    term = jnp.zeros((utts * frames, channels), jnp.float32)
    for tap in range(2):
        rows = x_wide[pl.ds(tap, utts * frames, stride=2), :].astype(jnp.bfloat16)
        term += jnp.dot(rows, cw_ref[tap], preferred_element_type=jnp.float32)
    term = term.reshape(utts, frames, channels)
    term_wide[...] = term
    term_half[...] = term.astype(jnp.bfloat16)
    sum_copies = [
        begin(
            remote(
                term_half.at[other_tensor(k)],
                arrived.at[k - 1],
                sum_send.at[k - 1],
                sum_recv.at[k - 1],
                tensor=other_tensor(k),
            )
        )
        for k in range(1, tensors)
    ]

    local.wait()
    for copy in tap_copies:
        copy.wait_recv()

    core = lax.rem(seq, 2)
    sibling = seq + 1 - 2 * core
    ups, downs = chips // 2, (chips - 1) // 2
    split = dps // 2

    def block_of(hop, part):
        index = lax.rem(seq + 2 * hop + seqs, seqs)
        if part is None:
            return taps_ref.at[:, index]
        return taps_ref.at[pl.ds(part * split, split), index]

    def pass_block(slot, hop, part=None):
        block = block_of(hop, part)
        return begin(
            remote(block, block, pair_send.at[slot], pair_recv.at[slot], seq=sibling)
        )

    def ring(slot, hop, direction, part=None):
        block = block_of(hop, part)
        return begin(
            remote(
                block,
                block,
                ring_send.at[slot],
                ring_recv.at[slot],
                seq=other_seq(2 * direction),
            )
        )

    up = [ring(0, 0, 1)]
    down = [ring(ups, 0, -1)]
    passed = {0: [pass_block(0, 0)]}

    def advance(step):
        last = step == ups
        up[step - 1].wait_recv()
        if not last:
            up.append(ring(step, -step, 1, 0 if step == ups - 1 else None))
        down[step - 1].wait_recv()
        if not last:
            down.append(ring(ups + step, step, -1, 1 if step == ups - 1 else None))
        if last:
            passed[-step] = [pass_block(step, -step, 0), pass_block(ups + step, -step, 1)]
        else:
            passed[-step] = [pass_block(step, -step)]
            passed[step] = [pass_block(ups + step, step)]

    summed = term_wide[tensor]
    for k, copy in enumerate(sum_copies):
        copy.wait_recv()
        summed = summed + arrived[k].astype(jnp.float32)
    row_mean = jnp.mean(summed, axis=-1, keepdims=True)
    row_square = jnp.mean(summed * summed, axis=-1, keepdims=True)
    normed = (summed - row_mean) * lax.rsqrt(row_square - row_mean * row_mean + ln_eps)
    feat[tensor] = exact_gelu(normed).astype(jnp.bfloat16)
    feat_copies = [
        begin(
            remote(
                feat.at[tensor],
                feat.at[tensor],
                feat_send.at[k - 1],
                feat_recv.at[k - 1],
                tensor=other_tensor(k),
            )
        )
        for k in range(1, tensors)
    ]
    for copy in loads[2:]:
        copy.wait()
    is_masked = (
        jnp.concatenate(
            [frame_mask(starts_ref[u : u + 1], seq * frames, frames) for u in range(utts)], axis=0
        )
        > 0
    )
    for copy in feat_copies:
        copy.wait_recv()
    features = feat[...].reshape(utts * frames, channels)
    embed = embed_ref[...].astype(jnp.float32)
    hidden[...] = jnp.zeros_like(hidden)
    for group in range(dps):
        here = slice(group * inner, (group + 1) * inner)
        projected = lax.dot_general(
            features,
            pw_ref[here, :],
            (((1,), (1,)), ((), ())),
            preferred_element_type=jnp.float32,
        )
        chosen = jnp.where(is_masked, embed[:, here], projected)
        hidden[group, :, :, :inner] = chosen.astype(jnp.bfloat16).reshape(utts, frames, inner)
    mine = pl.ds(dp * utts, utts)
    win_copies = []
    for k in range(dps):
        for side in (-1, 0, 1):
            slot = 3 * k + side + 1
            if k == 0 and side == 0:
                continue
            win_copies.append(
                begin(
                    remote(
                        hidden.at[other_dp(k)],
                        win_ref.at[mine, 1 - side],
                        win_send.at[slot],
                        win_recv.at[slot],
                        dp=other_dp(k),
                        seq=other_seq(side),
                    )
                )
            )
    win_ref[mine, 1] = hidden[dp]
    advance(1)
    local_codes.wait()
    for copy in code_copies:
        copy.wait_recv()
    for block in range(seqs):
        choice[:, block * frames : (block + 1) * frames] = codes_ref[block]
    entries, width = book_ref.shape[1:]
    half = choice.shape[1] // 2

    def make_targets(part):
        here = slice(part * half, (part + 1) * half)
        for qgroup in range(book_ref.shape[0]):
            row = lax.broadcasted_iota(jnp.int32, (entries, half), 0)
            onehot = jnp.where(row == choice[qgroup : qgroup + 1, here], 1.0, 0.0)
            codevec[:, qgroup * width : (qgroup + 1) * width] = lax.dot_general(
                onehot.astype(jnp.bfloat16),
                book_ref[qgroup],
                (((0,), (0,)), ((), ())),
                preferred_element_type=jnp.float32,
            ).astype(jnp.bfloat16)
        made = jnp.dot(codevec[...], qw_ref[...], preferred_element_type=jnp.float32)
        made = made.astype(jnp.bfloat16)
        targets_ref[here, :] = made
        made = made.astype(jnp.float32)
        norm = jnp.sum(made * made, axis=-1, keepdims=True)
        norms_ref[:, here] = jnp.transpose(jnp.broadcast_to(norm, (half, LANES)))[:1]

    make_targets(0)
    advance(2)
    for copy in win_copies:
        copy.wait_recv()

    @pl.when(seq == 0)
    def low_edge():
        win_ref[:, 0] = jnp.zeros_like(win_ref[:, 0])

    @pl.when(seq == seqs - 1)
    def high_edge():
        win_ref[:, 2] = jnp.zeros_like(win_ref[:, 2])

    kept = xc.shape[1]
    acc[...] = jnp.zeros_like(acc)
    wc[...] = jnp.zeros_like(wc)

    @pl.loop(0, dps * utts)
    def shift_copies(u):
        xf[...] = win_ref[u].reshape(xf.shape).astype(jnp.float32)
        for j in range(SHIFTS):
            xc[u, :, j * LANES : (j + 1) * LANES] = xf[j : j + kept, :].astype(jnp.bfloat16)

    span = acc.shape[1]
    joint = 4
    run = wc.shape[1]

    def conv_block(hop):
        for copy in passed[hop]:
            copy.wait_recv()
        chip = lax.div(lax.rem(seq - core + 2 * hop + seqs, seqs), 2)
        lane = pl.multiple_of(lax.rem(chip, 4) * run, run)
        base = lax.div(chip, 4) * SHIFTS
        for pair in range(dps // 2):
            for side in range(2):
                for i in range(4):
                    wc[
                        pair, i * LANES : i * LANES + inner, side * LANES : side * LANES + inner
                    ] = taps_ref[2 * pair + side, 2 * chip + i // 2, i % 2]

        @pl.loop(0, dps * utts // joint)
        def multiply(chunk):
            here = pl.ds(chunk * joint, joint)
            total = acc[here]
            for pair in range(dps // 2):
                first = pl.multiple_of(base + 64 * pair, SHIFTS)
                window = xc[here, pl.ds(first, span), pl.ds(lane, run)]
                total += jnp.dot(
                    window.reshape(joint * span, run),
                    wc[pair],
                    preferred_element_type=jnp.float32,
                ).reshape(joint, span, 2 * LANES)
            acc[here] = total

    conv_block(0)
    conv_block(1)
    conv_block(-1)
    advance(3)
    conv_block(2)
    conv_block(-2)
    make_targets(1)
    conv_block(3)
    conv_block(-3)
    advance(4)
    conv_block(-4)

    @pl.loop(0, dps * utts)
    def mix(u):
        conv_out = acc[u, :frames, :LANES] + acc[u, span - frames :, LANES:]
        own = win_ref[u, 1].astype(jnp.float32)
        mixed[u] = (own + exact_gelu(conv_out)).astype(jnp.bfloat16)

    mix_copies = [
        begin(
            remote(
                mixed.at[pl.ds(other_dp(k) * utts, utts)],
                gathered.at[dp],
                mix_send.at[k - 1],
                mix_recv.at[k - 1],
                dp=other_dp(k),
            )
        )
        for k in range(1, dps)
    ]
    gathered[dp] = mixed[mine]
    for copy in mix_copies:
        copy.wait_recv()
    code_dim = fw_ref.shape[1]
    part_copies = []
    for k in range(tensors):
        there = other_tensor(k + 1)
        total = jnp.zeros((frames, code_dim), jnp.float32)
        for group in range(dps):
            rows = gathered[group, there][:, :inner]
            weights = fw_ref[group * inner : (group + 1) * inner, :]
            total += jnp.dot(rows, weights, preferred_element_type=jnp.float32)
        if k < tensors - 1:
            part_half[k] = total.astype(jnp.bfloat16)
            part_copies.append(
                begin(
                    remote(
                        part_half.at[k],
                        part_arrived.at[k],
                        part_send.at[k],
                        part_recv.at[k],
                        tensor=there,
                    )
                )
            )
    for k, copy in enumerate(part_copies):
        copy.wait_recv()
        total += part_arrived[k].astype(jnp.float32)
    context_ref[...] = total.astype(jnp.bfloat16)
    for copy in pending:
        copy.wait_send()


def main_stage(sizes, x, cw, pw, embed, starts, book, qw, fw, taps, codes):
    dps, seqs, tensors = sizes
    utts, frames = x.shape[0], x.shape[1] // 2
    channels = cw.shape[2]
    code_dim = fw.shape[1]
    per, _, inner, outer = taps.shape
    hops = seqs // 2
    span = frames + KERNEL // dps
    hbm = pl.BlockSpec(memory_space=pltpu.HBM)
    vmem = pl.BlockSpec(memory_space=pltpu.VMEM)
    dma = pltpu.SemaphoreType.DMA
    half = jnp.bfloat16

    def like(array):
        return pltpu.VMEM(array.shape, array.dtype)

    return pl.pallas_call(
        functools.partial(main_body, sizes),
        out_shape=(
            jax.ShapeDtypeStruct((frames, code_dim), half),
            jax.ShapeDtypeStruct((seqs * frames, code_dim), half),
            jax.ShapeDtypeStruct((1, seqs * frames), jnp.float32),
        ),
        in_specs=[hbm] * 10,
        out_specs=(vmem, vmem, vmem),
        scratch_shapes=[
            like(x),
            like(cw),
            like(pw),
            like(embed),
            like(starts),
            like(book),
            like(qw),
            like(fw),
            pltpu.VMEM((dps, seqs, per, inner, outer), half),
            pltpu.VMEM((seqs,) + codes.shape, codes.dtype),
            pltpu.VMEM((codes.shape[0], seqs * frames), codes.dtype),
            pltpu.VMEM((seqs * frames // 2, qw.shape[0]), half),
            pltpu.VMEM((2 * utts * frames, x.shape[2]), jnp.float32),
            pltpu.VMEM((utts, frames, channels), jnp.float32),
            pltpu.VMEM((utts, frames, channels), half),
            pltpu.VMEM((tensors - 1, frames, channels), half),
            pltpu.VMEM((utts, frames, channels), half),
            pltpu.VMEM((dps, utts, frames, LANES), half),
            pltpu.VMEM((utts * dps, 3, frames, LANES), half),
            pltpu.VMEM((3 * frames, LANES), jnp.float32),
            pltpu.VMEM((utts * dps, 3 * frames - SHIFTS, SHIFTS * LANES), half),
            pltpu.VMEM((dps // 2, 4 * LANES, 2 * LANES), half),
            pltpu.VMEM((utts * dps, span, 2 * LANES), jnp.float32),
            pltpu.VMEM((utts * dps, frames, LANES), half),
            pltpu.VMEM((dps, utts, frames, LANES), half),
            pltpu.VMEM((tensors - 1, frames, code_dim), half),
            pltpu.VMEM((tensors - 1, frames, code_dim), half),
            dma((8,)),
            dma((2,)),
            dma((seqs - 1,)),
            dma((seqs - 1,)),
            dma((dps - 1,)),
            dma((dps - 1,)),
            dma((hops,)),
            dma((hops,)),
            dma((hops + 1,)),
            dma((hops + 1,)),
            dma((tensors - 1,)),
            dma((tensors - 1,)),
            dma((tensors - 1,)),
            dma((tensors - 1,)),
            dma((3 * dps,)),
            dma((3 * dps,)),
            dma((dps - 1,)),
            dma((dps - 1,)),
            dma((tensors - 1,)),
            dma((tensors - 1,)),
        ],
        compiler_params=pltpu.CompilerParams(
            collective_id=0, has_side_effects=True, vmem_limit_bytes=44 * 2**20
        ),
    )(x, cw, pw, embed, starts, book, qw, fw, taps, codes)


def loss_body(c_ref, t_ref, tn_ref, ids_ref, starts_ref, o_ref, ids):
    context = c_ref[...]
    frames, negs = ids_ref.shape
    ids[...] = jnp.zeros_like(ids)
    ids[:, :negs] = ids_ref[...]
    first = pl.multiple_of(lax.axis_index("seq") * frames, frames)
    scores = lax.dot_general(
        context, t_ref[...], (((1,), (1,)), ((), ())), preferred_element_type=jnp.float32
    )
    wide = context.astype(jnp.float32)
    own = t_ref[pl.ds(first, frames), :].astype(jnp.float32)
    ctx_norm = jnp.sum(wide * wide, axis=-1, keepdims=True) + norm_eps
    own_norm = jnp.sum(own * own, axis=-1, keepdims=True) + norm_eps
    pos_dot = jnp.sum(wide * own, axis=-1, keepdims=True)
    positive = pos_dot * lax.rsqrt(ctx_norm * own_norm) / logit_temp
    logits = scores * lax.rsqrt(ctx_norm * (tn_ref[...] + norm_eps)) / logit_temp
    powers = jnp.exp(logits)
    chosen = ids[...]
    lane = chosen % LANES
    chunk = chosen // LANES
    picked = jnp.zeros((frames, LANES), jnp.float32)
    for c in range(powers.shape[1] // LANES):
        found = jnp.take_along_axis(
            powers[:, c * LANES : (c + 1) * LANES], lane, axis=1, mode="promise_in_bounds"
        )
        picked = jnp.where(chunk == c, found, picked)
    real = lax.broadcasted_iota(jnp.int32, picked.shape, 1) < negs
    negatives = jnp.sum(jnp.where(real, picked, 0.0), axis=-1, keepdims=True)
    loss = jnp.log(jnp.exp(positive) + negatives) - positive
    starts = starts_ref[pl.ds(lax.axis_index("tensor"), 1), :]
    o_ref[...] = jnp.where(frame_mask(starts, first, frames) > 0, loss, 0.0)


def losses(context, targets, norms, ids, starts):
    return pl.pallas_call(
        loss_body,
        out_shape=jax.ShapeDtypeStruct((ids.shape[0], 1), jnp.float32),
        scratch_shapes=[pltpu.VMEM((ids.shape[0], LANES), jnp.int32)],
        compiler_params=pltpu.CompilerParams(vmem_limit_bytes=24 * 2**20),
    )(context, targets, norms, ids, starts)


def on_device(
    feature_in,
    conv_weight,
    proj_weight,
    mask_embed,
    pos_weight,
    final_weight,
    codebook,
    quant_weight,
    mask_starts,
    code_choice,
    negative_ids,
):
    sizes = tuple(lax.axis_size(name) for name in ("dp", "seq", "tensor"))
    context, targets, norms = main_stage(
        sizes,
        feature_in,
        conv_weight,
        proj_weight.T,
        mask_embed.reshape(1, -1),
        mask_starts,
        codebook,
        quant_weight,
        final_weight,
        pos_weight,
        code_choice[0].T,
    )
    loss = losses(context, targets, norms, negative_ids[0], mask_starts)
    return loss.reshape(1, -1)


def solution(mesh):
    return jax.shard_map(
        on_device,
        mesh=mesh,
        in_specs=(
            P("dp", "seq", "tensor"),
            P(None, "tensor", None),
            P(None, "tensor"),
            P("tensor"),
            P(("dp", "seq"), "tensor", None, None),
            P("tensor", None),
            P(),
            P(),
            P("dp", None),
            P(("dp", "tensor"), "seq", None),
            P(("dp", "tensor"), "seq", None),
        ),
        out_specs=P(("dp", "tensor"), "seq"),
        check_vma=False,
    )
```

```python
import functools

import jax
import jax.numpy as jnp
from jax import lax
from jax.experimental import pallas as pl
from jax.experimental.pallas import tpu as pltpu
from jax.sharding import PartitionSpec as P

KERNEL = 128
MASK_LEN = 10
SHIFTS = 16
LANES = 128


ln_eps = 1e-05
norm_eps = 1e-06
logit_temp = 0.1


def exact_gelu(value):
    return 0.5 * value * (1.0 + lax.erf(value * (0.5**0.5)))


def remote(src, dst, send, recv, **coords):
    return pltpu.make_async_remote_copy(
        src_ref=src,
        dst_ref=dst,
        send_sem=send,
        recv_sem=recv,
        device_id=coords,
        device_id_type=pl.DeviceIdType.MESH,
    )


def greet(barrier, **coords):
    pl.semaphore_signal(
        barrier, inc=1, device_id=coords, device_id_type=pl.DeviceIdType.MESH
    )


def frame_mask(starts, first, frames):
    position = first + lax.broadcasted_iota(jnp.int32, (frames, starts.shape[1]), 0)
    inside = (position >= starts) & (position < starts + MASK_LEN)
    return jnp.max(jnp.where(inside, 1.0, 0.0), axis=-1, keepdims=True)


def main_body(
    sizes,
    x_hbm,
    cw_hbm,
    pw_hbm,
    embed_hbm,
    starts_hbm,
    book_hbm,
    qw_hbm,
    fw_hbm,
    taps_in,
    codes_in,
    powers_ref,
    positive_ref,
    targets_ref,
    norms_ref,
    x_in,
    cw_ref,
    pw_ref,
    embed_ref,
    starts_ref,
    book_ref,
    qw_ref,
    fw_ref,
    taps_ref,
    codes_ref,
    choice,
    codevec,
    x_wide,
    term_wide,
    term_half,
    arrived,
    feat,
    hidden,
    win_ref,
    xf,
    xc,
    wc,
    acc,
    mixed,
    gathered,
    part_half,
    part_arrived,
    load_sem,
    local_sem,
    code_send,
    code_recv,
    tap_send,
    tap_recv,
    ring_send,
    ring_recv,
    pair_send,
    pair_recv,
    sum_send,
    sum_recv,
    feat_send,
    feat_recv,
    win_send,
    win_recv,
    mix_send,
    mix_recv,
    part_send,
    part_recv,
):
    dps, seqs, tensors = sizes
    chips = seqs // 2
    dp, seq, tensor = (lax.axis_index(name) for name in ("dp", "seq", "tensor"))
    utts, frames, channels = term_wide.shape
    inner = taps_ref.shape[-1]

    def other_dp(k):
        return lax.rem(dp + k, dps)

    def other_seq(k):
        return lax.rem(seq + (k + seqs) % seqs, seqs)

    def other_tensor(k):
        return lax.rem(tensor + k, tensors)

    loads = [
        pltpu.make_async_copy(source, target, load_sem.at[index])
        for index, (source, target) in enumerate(
            (
                (x_hbm, x_in),
                (cw_hbm, cw_ref),
                (pw_hbm, pw_ref),
                (embed_hbm, embed_ref),
                (starts_hbm, starts_ref),
                (book_hbm, book_ref),
                (qw_hbm, qw_ref),
                (fw_hbm, fw_ref),
            )
        )
    ]
    for copy in loads:
        copy.start()
    local = pltpu.make_async_copy(taps_in.at[:, dp], taps_ref.at[dp, seq], local_sem.at[0])
    local.start()
    local_codes = pltpu.make_async_copy(codes_in, codes_ref.at[seq], local_sem.at[1])
    local_codes.start()

    barrier = pltpu.get_barrier_semaphore()
    for k in range(1, seqs):
        greet(barrier, seq=other_seq(k))
    for k in range(1, dps):
        for side in (-1, 0, 1):
            greet(barrier, dp=other_dp(k), seq=other_seq(side))
    for k in range(1, tensors):
        greet(barrier, tensor=other_tensor(k))
    pl.semaphore_wait(barrier, (seqs - 1) + 3 * (dps - 1) + (tensors - 1))

    pending = []

    def begin(copy):
        copy.start()
        pending.append(copy)
        return copy

    tap_copies = [
        begin(
            remote(
                taps_in.at[:, other_dp(k)],
                taps_ref.at[dp, seq],
                tap_send.at[k - 1],
                tap_recv.at[k - 1],
                dp=other_dp(k),
            )
        )
        for k in range(1, dps)
    ]
    code_copies = [
        begin(
            remote(
                codes_in,
                codes_ref.at[seq],
                code_send.at[k - 1],
                code_recv.at[k - 1],
                seq=other_seq(k),
            )
        )
        for k in range(1, seqs)
    ]

    loads[0].wait()
    loads[1].wait()
    x_wide[...] = x_in[...].reshape(x_wide.shape).astype(jnp.float32)
    term = jnp.zeros((utts * frames, channels), jnp.float32)
    for tap in range(2):
        rows = x_wide[pl.ds(tap, utts * frames, stride=2), :].astype(jnp.bfloat16)
        term += jnp.dot(rows, cw_ref[tap], preferred_element_type=jnp.float32)
    term = term.reshape(utts, frames, channels)
    term_wide[...] = term
    term_half[...] = term.astype(jnp.bfloat16)
    sum_copies = [
        begin(
            remote(
                term_half.at[other_tensor(k)],
                arrived.at[k - 1],
                sum_send.at[k - 1],
                sum_recv.at[k - 1],
                tensor=other_tensor(k),
            )
        )
        for k in range(1, tensors)
    ]

    local.wait()
    for copy in tap_copies:
        copy.wait_recv()

    core = lax.rem(seq, 2)
    sibling = seq + 1 - 2 * core
    ups, downs = chips // 2, (chips - 1) // 2
    split = dps // 2

    def block_of(hop, part):
        index = lax.rem(seq + 2 * hop + seqs, seqs)
        if part is None:
            return taps_ref.at[:, index]
        return taps_ref.at[pl.ds(part * split, split), index]

    def pass_block(slot, hop, part=None):
        block = block_of(hop, part)
        return begin(
            remote(block, block, pair_send.at[slot], pair_recv.at[slot], seq=sibling)
        )

    def ring(slot, hop, direction, part=None):
        block = block_of(hop, part)
        return begin(
            remote(
                block,
                block,
                ring_send.at[slot],
                ring_recv.at[slot],
                seq=other_seq(2 * direction),
            )
        )

    up = [ring(0, 0, 1)]
    down = [ring(ups, 0, -1)]
    passed = {0: [pass_block(0, 0)]}

    def advance(step):
        last = step == ups
        up[step - 1].wait_recv()
        if not last:
            up.append(ring(step, -step, 1, 0 if step == ups - 1 else None))
        down[step - 1].wait_recv()
        if not last:
            down.append(ring(ups + step, step, -1, 1 if step == ups - 1 else None))
        if last:
            passed[-step] = [pass_block(step, -step, 0), pass_block(ups + step, -step, 1)]
        else:
            passed[-step] = [pass_block(step, -step)]
            passed[step] = [pass_block(ups + step, step)]

    summed = term_wide[tensor]
    for k, copy in enumerate(sum_copies):
        copy.wait_recv()
        summed = summed + arrived[k].astype(jnp.float32)
    row_mean = jnp.mean(summed, axis=-1, keepdims=True)
    row_square = jnp.mean(summed * summed, axis=-1, keepdims=True)
    normed = (summed - row_mean) * lax.rsqrt(row_square - row_mean * row_mean + ln_eps)
    feat[tensor] = exact_gelu(normed).astype(jnp.bfloat16)
    feat_copies = [
        begin(
            remote(
                feat.at[tensor],
                feat.at[tensor],
                feat_send.at[k - 1],
                feat_recv.at[k - 1],
                tensor=other_tensor(k),
            )
        )
        for k in range(1, tensors)
    ]
    for copy in loads[2:]:
        copy.wait()
    is_masked = (
        jnp.concatenate(
            [frame_mask(starts_ref[u : u + 1], seq * frames, frames) for u in range(utts)], axis=0
        )
        > 0
    )
    for copy in feat_copies:
        copy.wait_recv()
    features = feat[...].reshape(utts * frames, channels)
    embed = embed_ref[...].astype(jnp.float32)
    hidden[...] = jnp.zeros_like(hidden)
    for group in range(dps):
        here = slice(group * inner, (group + 1) * inner)
        projected = lax.dot_general(
            features,
            pw_ref[here, :],
            (((1,), (1,)), ((), ())),
            preferred_element_type=jnp.float32,
        )
        chosen = jnp.where(is_masked, embed[:, here], projected)
        hidden[group, :, :, :inner] = chosen.astype(jnp.bfloat16).reshape(utts, frames, inner)
    mine = pl.ds(dp * utts, utts)
    win_copies = []
    for k in range(dps):
        for side in (-1, 0, 1):
            slot = 3 * k + side + 1
            if k == 0 and side == 0:
                continue
            win_copies.append(
                begin(
                    remote(
                        hidden.at[other_dp(k)],
                        win_ref.at[mine, 1 - side],
                        win_send.at[slot],
                        win_recv.at[slot],
                        dp=other_dp(k),
                        seq=other_seq(side),
                    )
                )
            )
    win_ref[mine, 1] = hidden[dp]
    advance(1)
    local_codes.wait()
    for copy in code_copies:
        copy.wait_recv()
    for block in range(seqs):
        choice[:, block * frames : (block + 1) * frames] = codes_ref[block]
    entries, width = book_ref.shape[1:]
    half = choice.shape[1] // 2

    def make_targets(part):
        here = slice(part * half, (part + 1) * half)
        for qgroup in range(book_ref.shape[0]):
            row = lax.broadcasted_iota(jnp.int32, (entries, half), 0)
            onehot = jnp.where(row == choice[qgroup : qgroup + 1, here], 1.0, 0.0)
            codevec[:, qgroup * width : (qgroup + 1) * width] = lax.dot_general(
                onehot.astype(jnp.bfloat16),
                book_ref[qgroup],
                (((0,), (0,)), ((), ())),
                preferred_element_type=jnp.float32,
            ).astype(jnp.bfloat16)
        made = jnp.dot(codevec[...], qw_ref[...], preferred_element_type=jnp.float32)
        made = made.astype(jnp.bfloat16)
        targets_ref[here, :] = made
        made = made.astype(jnp.float32)
        norm = jnp.sum(made * made, axis=-1, keepdims=True)
        norms_ref[:, here] = jnp.transpose(jnp.broadcast_to(norm, (half, LANES)))[:1]

    make_targets(0)
    advance(2)
    for copy in win_copies:
        copy.wait_recv()

    @pl.when(seq == 0)
    def low_edge():
        win_ref[:, 0] = jnp.zeros_like(win_ref[:, 0])

    @pl.when(seq == seqs - 1)
    def high_edge():
        win_ref[:, 2] = jnp.zeros_like(win_ref[:, 2])

    kept = xc.shape[1]
    acc[...] = jnp.zeros_like(acc)
    wc[...] = jnp.zeros_like(wc)

    @pl.loop(0, dps * utts)
    def shift_copies(u):
        xf[...] = win_ref[u].reshape(xf.shape).astype(jnp.float32)
        for j in range(SHIFTS):
            xc[u, :, j * LANES : (j + 1) * LANES] = xf[j : j + kept, :].astype(jnp.bfloat16)

    span = acc.shape[1]
    joint = 4
    run = wc.shape[1]

    def conv_block(hop):
        for copy in passed[hop]:
            copy.wait_recv()
        chip = lax.div(lax.rem(seq - core + 2 * hop + seqs, seqs), 2)
        lane = pl.multiple_of(lax.rem(chip, 4) * run, run)
        base = lax.div(chip, 4) * SHIFTS
        for pair in range(dps // 2):
            for side in range(2):
                for i in range(4):
                    wc[
                        pair, i * LANES : i * LANES + inner, side * LANES : side * LANES + inner
                    ] = taps_ref[2 * pair + side, 2 * chip + i // 2, i % 2]

        @pl.loop(0, dps * utts // joint)
        def multiply(chunk):
            here = pl.ds(chunk * joint, joint)
            total = acc[here]
            for pair in range(dps // 2):
                first = pl.multiple_of(base + 64 * pair, SHIFTS)
                window = xc[here, pl.ds(first, span), pl.ds(lane, run)]
                total += jnp.dot(
                    window.reshape(joint * span, run),
                    wc[pair],
                    preferred_element_type=jnp.float32,
                ).reshape(joint, span, 2 * LANES)
            acc[here] = total

    conv_block(0)
    conv_block(1)
    conv_block(-1)
    advance(3)
    conv_block(2)
    conv_block(-2)
    make_targets(1)
    conv_block(3)
    conv_block(-3)
    advance(4)
    conv_block(-4)

    @pl.loop(0, dps * utts)
    def mix(u):
        conv_out = acc[u, :frames, :LANES] + acc[u, span - frames :, LANES:]
        own = win_ref[u, 1].astype(jnp.float32)
        mixed[u] = (own + exact_gelu(conv_out)).astype(jnp.bfloat16)

    mix_copies = [
        begin(
            remote(
                mixed.at[pl.ds(other_dp(k) * utts, utts)],
                gathered.at[dp],
                mix_send.at[k - 1],
                mix_recv.at[k - 1],
                dp=other_dp(k),
            )
        )
        for k in range(1, dps)
    ]
    gathered[dp] = mixed[mine]
    for copy in mix_copies:
        copy.wait_recv()
    code_dim = fw_ref.shape[1]
    part_copies = []
    for k in range(tensors):
        there = other_tensor(k + 1)
        total = jnp.zeros((frames, code_dim), jnp.float32)
        for group in range(dps):
            rows = gathered[group, there][:, :inner]
            weights = fw_ref[group * inner : (group + 1) * inner, :]
            total += jnp.dot(rows, weights, preferred_element_type=jnp.float32)
        if k < tensors - 1:
            part_half[k] = total.astype(jnp.bfloat16)
            part_copies.append(
                begin(
                    remote(
                        part_half.at[k],
                        part_arrived.at[k],
                        part_send.at[k],
                        part_recv.at[k],
                        tensor=there,
                    )
                )
            )
    for k, copy in enumerate(part_copies):
        copy.wait_recv()
        total += part_arrived[k].astype(jnp.float32)
    context = total.astype(jnp.bfloat16)
    scores = lax.dot_general(
        context,
        targets_ref[...],
        (((1,), (1,)), ((), ())),
        preferred_element_type=jnp.float32,
    )
    wide = context.astype(jnp.float32)
    first = pl.multiple_of(seq * frames, frames)
    own = targets_ref[pl.ds(first, frames), :].astype(jnp.float32)
    ctx_norm = jnp.sum(wide * wide, axis=-1, keepdims=True) + norm_eps
    own_norm = jnp.sum(own * own, axis=-1, keepdims=True) + norm_eps
    pos_dot = jnp.sum(wide * own, axis=-1, keepdims=True)
    positive_ref[...] = pos_dot * lax.rsqrt(ctx_norm * own_norm) / logit_temp
    logits = scores * lax.rsqrt(ctx_norm * (norms_ref[...] + norm_eps)) / logit_temp
    powers_ref[...] = jnp.exp(logits)
    for copy in pending:
        copy.wait_send()


def main_stage(sizes, x, cw, pw, embed, starts, book, qw, fw, taps, codes):
    dps, seqs, tensors = sizes
    utts, frames = x.shape[0], x.shape[1] // 2
    channels = cw.shape[2]
    code_dim = fw.shape[1]
    per, _, inner, outer = taps.shape
    hops = seqs // 2
    span = frames + KERNEL // dps
    hbm = pl.BlockSpec(memory_space=pltpu.HBM)
    vmem = pl.BlockSpec(memory_space=pltpu.VMEM)
    dma = pltpu.SemaphoreType.DMA
    half = jnp.bfloat16

    def like(array):
        return pltpu.VMEM(array.shape, array.dtype)

    return pl.pallas_call(
        functools.partial(main_body, sizes),
        out_shape=(
            jax.ShapeDtypeStruct((frames, seqs * frames), jnp.float32),
            jax.ShapeDtypeStruct((frames, 1), jnp.float32),
        ),
        in_specs=[hbm] * 10,
        out_specs=(vmem, vmem),
        scratch_shapes=[
            pltpu.VMEM((seqs * frames, code_dim), half),
            pltpu.VMEM((1, seqs * frames), jnp.float32),
            like(x),
            like(cw),
            like(pw),
            like(embed),
            like(starts),
            like(book),
            like(qw),
            like(fw),
            pltpu.VMEM((dps, seqs, per, inner, outer), half),
            pltpu.VMEM((seqs,) + codes.shape, codes.dtype),
            pltpu.VMEM((codes.shape[0], seqs * frames), codes.dtype),
            pltpu.VMEM((seqs * frames // 2, qw.shape[0]), half),
            pltpu.VMEM((2 * utts * frames, x.shape[2]), jnp.float32),
            pltpu.VMEM((utts, frames, channels), jnp.float32),
            pltpu.VMEM((utts, frames, channels), half),
            pltpu.VMEM((tensors - 1, frames, channels), half),
            pltpu.VMEM((utts, frames, channels), half),
            pltpu.VMEM((dps, utts, frames, LANES), half),
            pltpu.VMEM((utts * dps, 3, frames, LANES), half),
            pltpu.VMEM((3 * frames, LANES), jnp.float32),
            pltpu.VMEM((utts * dps, 3 * frames - SHIFTS, SHIFTS * LANES), half),
            pltpu.VMEM((dps // 2, 4 * LANES, 2 * LANES), half),
            pltpu.VMEM((utts * dps, span, 2 * LANES), jnp.float32),
            pltpu.VMEM((utts * dps, frames, LANES), half),
            pltpu.VMEM((dps, utts, frames, LANES), half),
            pltpu.VMEM((tensors - 1, frames, code_dim), half),
            pltpu.VMEM((tensors - 1, frames, code_dim), half),
            dma((8,)),
            dma((2,)),
            dma((seqs - 1,)),
            dma((seqs - 1,)),
            dma((dps - 1,)),
            dma((dps - 1,)),
            dma((hops,)),
            dma((hops,)),
            dma((hops + 1,)),
            dma((hops + 1,)),
            dma((tensors - 1,)),
            dma((tensors - 1,)),
            dma((tensors - 1,)),
            dma((tensors - 1,)),
            dma((3 * dps,)),
            dma((3 * dps,)),
            dma((dps - 1,)),
            dma((dps - 1,)),
            dma((tensors - 1,)),
            dma((tensors - 1,)),
        ],
        compiler_params=pltpu.CompilerParams(
            collective_id=0, has_side_effects=True, vmem_limit_bytes=60 * 2**20
        ),
    )(x, cw, pw, embed, starts, book, qw, fw, taps, codes)


def loss_body(powers_ref, positive_ref, ids_ref, starts_ref, o_ref, ids):
    frames, negs = ids_ref.shape
    ids[...] = jnp.zeros_like(ids)
    ids[:, :negs] = ids_ref[...]
    powers = powers_ref[...]
    positive = positive_ref[...]
    chosen = ids[...]
    lane = chosen % LANES
    chunk = chosen // LANES
    picked = jnp.zeros((frames, LANES), jnp.float32)
    for c in range(powers.shape[1] // LANES):
        found = jnp.take_along_axis(
            powers[:, c * LANES : (c + 1) * LANES], lane, axis=1, mode="promise_in_bounds"
        )
        picked = jnp.where(chunk == c, found, picked)
    real = lax.broadcasted_iota(jnp.int32, picked.shape, 1) < negs
    negatives = jnp.sum(jnp.where(real, picked, 0.0), axis=-1, keepdims=True)
    loss = jnp.log(jnp.exp(positive) + negatives) - positive
    starts = starts_ref[pl.ds(lax.axis_index("tensor"), 1), :]
    o_ref[...] = jnp.where(frame_mask(starts, lax.axis_index("seq") * frames, frames) > 0, loss, 0.0)


def losses(powers, positive, ids, starts):
    return pl.pallas_call(
        loss_body,
        out_shape=jax.ShapeDtypeStruct((ids.shape[0], 1), jnp.float32),
        scratch_shapes=[pltpu.VMEM((ids.shape[0], LANES), jnp.int32)],
        compiler_params=pltpu.CompilerParams(vmem_limit_bytes=24 * 2**20),
    )(powers, positive, ids, starts)


def on_device(
    feature_in,
    conv_weight,
    proj_weight,
    mask_embed,
    pos_weight,
    final_weight,
    codebook,
    quant_weight,
    mask_starts,
    code_choice,
    negative_ids,
):
    sizes = tuple(lax.axis_size(name) for name in ("dp", "seq", "tensor"))
    powers, positive = main_stage(
        sizes,
        feature_in,
        conv_weight,
        proj_weight.T,
        mask_embed.reshape(1, -1),
        mask_starts,
        codebook,
        quant_weight,
        final_weight,
        pos_weight,
        code_choice[0].T,
    )
    loss = losses(powers, positive, negative_ids[0], mask_starts)
    return loss.reshape(1, -1)


def solution(mesh):
    return jax.shard_map(
        on_device,
        mesh=mesh,
        in_specs=(
            P("dp", "seq", "tensor"),
            P(None, "tensor", None),
            P(None, "tensor"),
            P("tensor"),
            P(("dp", "seq"), "tensor", None, None),
            P("tensor", None),
            P(),
            P(),
            P("dp", None),
            P(("dp", "tensor"), "seq", None),
            P(("dp", "tensor"), "seq", None),
        ),
        out_specs=P(("dp", "tensor"), "seq"),
        check_vma=False,
    )
```

```python
import functools

import jax
import jax.numpy as jnp
from jax import lax
from jax.experimental import pallas as pl
from jax.experimental.pallas import tpu as pltpu
from jax.sharding import PartitionSpec as P

KERNEL = 128
MASK_LEN = 10
SHIFTS = 16
LANES = 128


ln_eps = 1e-05
norm_eps = 1e-06
logit_temp = 0.1


def exact_gelu(value):
    return 0.5 * value * (1.0 + lax.erf(value * (0.5**0.5)))


def remote(src, dst, send, recv, **coords):
    return pltpu.make_async_remote_copy(
        src_ref=src,
        dst_ref=dst,
        send_sem=send,
        recv_sem=recv,
        device_id=coords,
        device_id_type=pl.DeviceIdType.MESH,
    )


def greet(barrier, **coords):
    pl.semaphore_signal(
        barrier, inc=1, device_id=coords, device_id_type=pl.DeviceIdType.MESH
    )


def frame_mask(starts, first, frames):
    position = first + lax.broadcasted_iota(jnp.int32, (frames, starts.shape[1]), 0)
    inside = (position >= starts) & (position < starts + MASK_LEN)
    return jnp.max(jnp.where(inside, 1.0, 0.0), axis=-1, keepdims=True)


def main_body(
    sizes,
    x_hbm,
    cw_hbm,
    pw_hbm,
    embed_hbm,
    starts_hbm,
    book_hbm,
    qw_hbm,
    fw_hbm,
    taps_in,
    codes_in,
    powers_ref,
    positive_ref,
    targets_ref,
    norms_ref,
    x_in,
    cw_ref,
    pw_ref,
    embed_ref,
    starts_ref,
    book_ref,
    qw_ref,
    fw_ref,
    taps_ref,
    codes_ref,
    choice,
    codevec,
    x_wide,
    term_wide,
    term_half,
    arrived,
    feat,
    hidden,
    win_ref,
    xf,
    xc,
    wc,
    acc,
    mixed,
    gathered,
    joined,
    load_sem,
    local_sem,
    code_send,
    code_recv,
    tap_send,
    tap_recv,
    ring_send,
    ring_recv,
    pair_send,
    pair_recv,
    sum_send,
    sum_recv,
    feat_send,
    feat_recv,
    win_send,
    win_recv,
    mix_send,
    mix_recv,
    final_send,
    final_recv,
    side_send,
    side_recv,
):
    dps, seqs, tensors = sizes
    chips = seqs // 2
    dp, seq, tensor = (lax.axis_index(name) for name in ("dp", "seq", "tensor"))
    utts, frames, channels = term_wide.shape
    inner = taps_ref.shape[-1]

    def other_dp(k):
        return lax.rem(dp + k, dps)

    def other_seq(k):
        return lax.rem(seq + (k + seqs) % seqs, seqs)

    def other_tensor(k):
        return lax.rem(tensor + k, tensors)

    loads = [
        pltpu.make_async_copy(source, target, load_sem.at[index])
        for index, (source, target) in enumerate(
            (
                (x_hbm, x_in),
                (cw_hbm, cw_ref),
                (pw_hbm, pw_ref),
                (embed_hbm, embed_ref),
                (starts_hbm, starts_ref),
                (book_hbm, book_ref),
                (qw_hbm, qw_ref),
            )
        )
    ]
    for copy in loads:
        copy.start()
    local = pltpu.make_async_copy(taps_in.at[:, dp], taps_ref.at[dp, seq], local_sem.at[0])
    local.start()
    local_codes = pltpu.make_async_copy(codes_in, codes_ref.at[seq], local_sem.at[1])
    local_codes.start()
    local_final = pltpu.make_async_copy(fw_hbm, fw_ref.at[tensor], local_sem.at[2])
    local_final.start()

    barrier = pltpu.get_barrier_semaphore()
    for k in range(1, seqs):
        greet(barrier, seq=other_seq(k))
    for k in range(1, dps):
        for side in (-1, 0, 1):
            greet(barrier, dp=other_dp(k), seq=other_seq(side))
    for k in range(1, tensors):
        for m in range(dps):
            greet(barrier, tensor=other_tensor(k), dp=other_dp(m))
    pl.semaphore_wait(barrier, (seqs - 1) + 3 * (dps - 1) + (tensors - 1) * dps)

    pending = []

    def begin(copy):
        copy.start()
        pending.append(copy)
        return copy

    tap_copies = [
        begin(
            remote(
                taps_in.at[:, other_dp(k)],
                taps_ref.at[dp, seq],
                tap_send.at[k - 1],
                tap_recv.at[k - 1],
                dp=other_dp(k),
            )
        )
        for k in range(1, dps)
    ]
    code_copies = [
        begin(
            remote(
                codes_in,
                codes_ref.at[seq],
                code_send.at[k - 1],
                code_recv.at[k - 1],
                seq=other_seq(k),
            )
        )
        for k in range(1, seqs)
    ]

    loads[0].wait()
    loads[1].wait()
    x_wide[...] = x_in[...].reshape(x_wide.shape).astype(jnp.float32)
    term = jnp.zeros((utts * frames, channels), jnp.float32)
    for tap in range(2):
        rows = x_wide[pl.ds(tap, utts * frames, stride=2), :].astype(jnp.bfloat16)
        term += jnp.dot(rows, cw_ref[tap], preferred_element_type=jnp.float32)
    term = term.reshape(utts, frames, channels)
    term_wide[...] = term
    term_half[...] = term.astype(jnp.bfloat16)
    sum_copies = [
        begin(
            remote(
                term_half.at[other_tensor(k)],
                arrived.at[k - 1],
                sum_send.at[k - 1],
                sum_recv.at[k - 1],
                tensor=other_tensor(k),
            )
        )
        for k in range(1, tensors)
    ]

    local.wait()
    for copy in tap_copies:
        copy.wait_recv()

    core = lax.rem(seq, 2)
    sibling = seq + 1 - 2 * core
    ups, downs = chips // 2, (chips - 1) // 2
    split = dps // 2

    def block_of(hop, part):
        index = lax.rem(seq + 2 * hop + seqs, seqs)
        if part is None:
            return taps_ref.at[:, index]
        return taps_ref.at[pl.ds(part * split, split), index]

    def pass_block(slot, hop, part=None):
        block = block_of(hop, part)
        return begin(
            remote(block, block, pair_send.at[slot], pair_recv.at[slot], seq=sibling)
        )

    def ring(slot, hop, direction, part=None):
        block = block_of(hop, part)
        return begin(
            remote(
                block,
                block,
                ring_send.at[slot],
                ring_recv.at[slot],
                seq=other_seq(2 * direction),
            )
        )

    up = [ring(0, 0, 1)]
    down = [ring(ups, 0, -1)]
    passed = {0: [pass_block(0, 0)]}

    def advance(step):
        last = step == ups
        up[step - 1].wait_recv()
        if not last:
            up.append(ring(step, -step, 1, 0 if step == ups - 1 else None))
        down[step - 1].wait_recv()
        if not last:
            down.append(ring(ups + step, step, -1, 1 if step == ups - 1 else None))
        if last:
            passed[-step] = [pass_block(step, -step, 0), pass_block(ups + step, -step, 1)]
        else:
            passed[-step] = [pass_block(step, -step)]
            passed[step] = [pass_block(ups + step, step)]

    summed = term_wide[tensor]
    for k, copy in enumerate(sum_copies):
        copy.wait_recv()
        summed = summed + arrived[k].astype(jnp.float32)
    row_mean = jnp.mean(summed, axis=-1, keepdims=True)
    row_square = jnp.mean(summed * summed, axis=-1, keepdims=True)
    normed = (summed - row_mean) * lax.rsqrt(row_square - row_mean * row_mean + ln_eps)
    feat[tensor] = exact_gelu(normed).astype(jnp.bfloat16)
    feat_copies = [
        begin(
            remote(
                feat.at[tensor],
                feat.at[tensor],
                feat_send.at[k - 1],
                feat_recv.at[k - 1],
                tensor=other_tensor(k),
            )
        )
        for k in range(1, tensors)
    ]
    final_copies = [
        begin(
            remote(
                fw_hbm.at[core],
                fw_ref.at[tensor, core],
                final_send.at[k - 1],
                final_recv.at[k - 1],
                tensor=other_tensor(k),
            )
        )
        for k in range(1, tensors)
    ]
    for copy in loads[2:]:
        copy.wait()
    is_masked = (
        jnp.concatenate(
            [frame_mask(starts_ref[u : u + 1], seq * frames, frames) for u in range(utts)], axis=0
        )
        > 0
    )
    for copy in feat_copies:
        copy.wait_recv()
    features = feat[...].reshape(utts * frames, channels)
    embed = embed_ref[...].astype(jnp.float32)
    hidden[...] = jnp.zeros_like(hidden)
    for group in range(dps):
        here = slice(group * inner, (group + 1) * inner)
        projected = lax.dot_general(
            features,
            pw_ref[here, :],
            (((1,), (1,)), ((), ())),
            preferred_element_type=jnp.float32,
        )
        chosen = jnp.where(is_masked, embed[:, here], projected)
        hidden[group, :, :, :inner] = chosen.astype(jnp.bfloat16).reshape(utts, frames, inner)
    mine = pl.ds(dp * utts, utts)
    win_copies = []
    for k in range(dps):
        for side in (-1, 0, 1):
            slot = 3 * k + side + 1
            if k == 0 and side == 0:
                continue
            win_copies.append(
                begin(
                    remote(
                        hidden.at[other_dp(k)],
                        win_ref.at[mine, 1 - side],
                        win_send.at[slot],
                        win_recv.at[slot],
                        dp=other_dp(k),
                        seq=other_seq(side),
                    )
                )
            )
    win_ref[mine, 1] = hidden[dp]
    advance(1)
    local_codes.wait()
    for copy in code_copies:
        copy.wait_recv()
    for block in range(seqs):
        choice[:, block * frames : (block + 1) * frames] = codes_ref[block]
    entries, width = book_ref.shape[1:]
    half = choice.shape[1] // 2

    def make_targets(part):
        here = slice(part * half, (part + 1) * half)
        for qgroup in range(book_ref.shape[0]):
            row = lax.broadcasted_iota(jnp.int32, (entries, half), 0)
            onehot = jnp.where(row == choice[qgroup : qgroup + 1, here], 1.0, 0.0)
            codevec[:, qgroup * width : (qgroup + 1) * width] = lax.dot_general(
                onehot.astype(jnp.bfloat16),
                book_ref[qgroup],
                (((0,), (0,)), ((), ())),
                preferred_element_type=jnp.float32,
            ).astype(jnp.bfloat16)
        made = jnp.dot(codevec[...], qw_ref[...], preferred_element_type=jnp.float32)
        made = made.astype(jnp.bfloat16)
        targets_ref[here, :] = made
        made = made.astype(jnp.float32)
        norm = jnp.sum(made * made, axis=-1, keepdims=True)
        norms_ref[:, here] = jnp.transpose(jnp.broadcast_to(norm, (half, LANES)))[:1]

    make_targets(0)
    advance(2)
    for copy in win_copies:
        copy.wait_recv()

    @pl.when(seq == 0)
    def low_edge():
        win_ref[:, 0] = jnp.zeros_like(win_ref[:, 0])

    @pl.when(seq == seqs - 1)
    def high_edge():
        win_ref[:, 2] = jnp.zeros_like(win_ref[:, 2])

    kept = xc.shape[1]
    acc[...] = jnp.zeros_like(acc)
    wc[...] = jnp.zeros_like(wc)

    @pl.loop(0, dps * utts)
    def shift_copies(u):
        xf[...] = win_ref[u].reshape(xf.shape).astype(jnp.float32)
        for j in range(SHIFTS):
            xc[u, :, j * LANES : (j + 1) * LANES] = xf[j : j + kept, :].astype(jnp.bfloat16)

    span = acc.shape[1]
    run = wc.shape[1]

    def load_block(hop):
        for copy in passed[hop]:
            copy.wait_recv()
        chip = lax.div(lax.rem(seq - core + 2 * hop + seqs, seqs), 2)
        lane = pl.multiple_of(lax.rem(chip, 4) * run, run)
        base = lax.div(chip, 4) * SHIFTS
        for pair in range(dps // 2):
            for side in range(2):
                for i in range(4):
                    wc[
                        pair, i * LANES : i * LANES + inner, side * LANES : side * LANES + inner
                    ] = taps_ref[2 * pair + side, 2 * chip + i // 2, i % 2]
        return lane, base

    def chunk_total(chunk, lane, base):
        here = pl.ds(chunk * utts, utts)
        total = acc[here]
        for pair in range(dps // 2):
            first = pl.multiple_of(base + 64 * pair, SHIFTS)
            window = xc[here, pl.ds(first, span), pl.ds(lane, run)]
            total += jnp.dot(
                window.reshape(utts * span, run),
                wc[pair],
                preferred_element_type=jnp.float32,
            ).reshape(utts, span, 2 * LANES)
        return total

    def conv_block(hop):
        lane, base = load_block(hop)

        @pl.loop(0, dps)
        def multiply(chunk):
            acc[pl.ds(chunk * utts, utts)] = chunk_total(chunk, lane, base)

    conv_block(0)
    conv_block(1)
    conv_block(-1)
    advance(3)
    conv_block(2)
    conv_block(-2)
    make_targets(1)
    conv_block(3)
    final_passes = []
    for k, copy in enumerate(final_copies):
        copy.wait_recv()
        block = fw_ref.at[lax.rem(tensor + tensors - k - 1, tensors), core]
        final_passes.append(
            begin(remote(block, block, side_send.at[k], side_recv.at[k], seq=sibling))
        )
    advance(4)
    conv_block(-3)

    lane, base = load_block(-4)
    mix_copies = []
    for k in (1, 2, 3, 0):
        chunk = other_dp(k)
        total = chunk_total(chunk, lane, base)
        conv_out = total[:, :frames, :LANES] + total[:, span - frames :, LANES:]
        own = win_ref[pl.ds(chunk * utts, utts), 1].astype(jnp.float32)
        mixed[pl.ds(chunk * utts, utts)] = (own + exact_gelu(conv_out)).astype(jnp.bfloat16)
        for m in (2, 1, 3, 0):
            if k == 0 and m == 0:
                continue
            slot = k * tensors + m
            mix_copies.append(
                begin(
                    remote(
                        mixed.at[chunk * utts + other_tensor(m)],
                        gathered.at[tensor * dps + dp],
                        mix_send.at[slot],
                        mix_recv.at[slot],
                        dp=chunk,
                        tensor=other_tensor(m),
                    )
                )
            )
    gathered[tensor * dps + dp] = mixed[dp * utts + tensor]
    local_final.wait()
    for copy in final_passes + mix_copies:
        copy.wait_recv()
    code_dim = fw_ref.shape[-1]
    for group in range(tensors * dps):
        joined[:, group * inner : (group + 1) * inner] = gathered[group][:, :inner]
    total = jnp.dot(
        joined[...],
        fw_ref[...].reshape(joined.shape[1], code_dim),
        preferred_element_type=jnp.float32,
    )
    context = total.astype(jnp.bfloat16)
    scores = lax.dot_general(
        context,
        targets_ref[...],
        (((1,), (1,)), ((), ())),
        preferred_element_type=jnp.float32,
    )
    wide = context.astype(jnp.float32)
    first = pl.multiple_of(seq * frames, frames)
    own = targets_ref[pl.ds(first, frames), :].astype(jnp.float32)
    ctx_norm = jnp.sum(wide * wide, axis=-1, keepdims=True) + norm_eps
    own_norm = jnp.sum(own * own, axis=-1, keepdims=True) + norm_eps
    pos_dot = jnp.sum(wide * own, axis=-1, keepdims=True)
    positive_ref[...] = pos_dot * lax.rsqrt(ctx_norm * own_norm) / logit_temp
    logits = scores * lax.rsqrt(ctx_norm * (norms_ref[...] + norm_eps)) / logit_temp
    powers_ref[...] = jnp.exp(logits)
    for copy in pending:
        copy.wait_send()


def main_stage(sizes, x, cw, pw, embed, starts, book, qw, fw, taps, codes):
    dps, seqs, tensors = sizes
    utts, frames = x.shape[0], x.shape[1] // 2
    channels = cw.shape[2]
    code_dim = fw.shape[2]
    per, _, inner, outer = taps.shape
    hops = seqs // 2
    span = frames + KERNEL // dps
    hbm = pl.BlockSpec(memory_space=pltpu.HBM)
    vmem = pl.BlockSpec(memory_space=pltpu.VMEM)
    dma = pltpu.SemaphoreType.DMA
    half = jnp.bfloat16

    def like(array):
        return pltpu.VMEM(array.shape, array.dtype)

    return pl.pallas_call(
        functools.partial(main_body, sizes),
        out_shape=(
            jax.ShapeDtypeStruct((frames, seqs * frames), jnp.float32),
            jax.ShapeDtypeStruct((frames, 1), jnp.float32),
        ),
        in_specs=[hbm] * 10,
        out_specs=(vmem, vmem),
        scratch_shapes=[
            pltpu.VMEM((seqs * frames, code_dim), half),
            pltpu.VMEM((1, seqs * frames), jnp.float32),
            like(x),
            like(cw),
            like(pw),
            like(embed),
            like(starts),
            like(book),
            like(qw),
            pltpu.VMEM((tensors,) + fw.shape, half),
            pltpu.VMEM((dps, seqs, per, inner, outer), half),
            pltpu.VMEM((seqs,) + codes.shape, codes.dtype),
            pltpu.VMEM((codes.shape[0], seqs * frames), codes.dtype),
            pltpu.VMEM((seqs * frames // 2, qw.shape[0]), half),
            pltpu.VMEM((2 * utts * frames, x.shape[2]), jnp.float32),
            pltpu.VMEM((utts, frames, channels), jnp.float32),
            pltpu.VMEM((utts, frames, channels), half),
            pltpu.VMEM((tensors - 1, frames, channels), half),
            pltpu.VMEM((utts, frames, channels), half),
            pltpu.VMEM((dps, utts, frames, LANES), half),
            pltpu.VMEM((utts * dps, 3, frames, LANES), half),
            pltpu.VMEM((3 * frames, LANES), jnp.float32),
            pltpu.VMEM((utts * dps, 3 * frames - SHIFTS, SHIFTS * LANES), half),
            pltpu.VMEM((dps // 2, 4 * LANES, 2 * LANES), half),
            pltpu.VMEM((utts * dps, span, 2 * LANES), jnp.float32),
            pltpu.VMEM((utts * dps, frames, LANES), half),
            pltpu.VMEM((tensors * dps, frames, LANES), half),
            pltpu.VMEM((frames, tensors * dps * inner), half),
            dma((7,)),
            dma((3,)),
            dma((seqs - 1,)),
            dma((seqs - 1,)),
            dma((dps - 1,)),
            dma((dps - 1,)),
            dma((hops,)),
            dma((hops,)),
            dma((hops + 1,)),
            dma((hops + 1,)),
            dma((tensors - 1,)),
            dma((tensors - 1,)),
            dma((tensors - 1,)),
            dma((tensors - 1,)),
            dma((3 * dps,)),
            dma((3 * dps,)),
            dma((dps * tensors,)),
            dma((dps * tensors,)),
            dma((tensors - 1,)),
            dma((tensors - 1,)),
            dma((tensors - 1,)),
            dma((tensors - 1,)),
        ],
        compiler_params=pltpu.CompilerParams(
            collective_id=0, has_side_effects=True, vmem_limit_bytes=60 * 2**20
        ),
    )(x, cw, pw, embed, starts, book, qw, fw, taps, codes)


def loss_body(powers_ref, positive_ref, ids_ref, starts_ref, o_ref, ids):
    frames, negs = ids_ref.shape
    ids[...] = jnp.zeros_like(ids)
    ids[:, :negs] = ids_ref[...]
    powers = powers_ref[...]
    positive = positive_ref[...]
    chosen = ids[...]
    lane = chosen % LANES
    chunk = chosen // LANES
    picked = jnp.zeros((frames, LANES), jnp.float32)
    for c in range(powers.shape[1] // LANES):
        found = jnp.take_along_axis(
            powers[:, c * LANES : (c + 1) * LANES], lane, axis=1, mode="promise_in_bounds"
        )
        picked = jnp.where(chunk == c, found, picked)
    real = lax.broadcasted_iota(jnp.int32, picked.shape, 1) < negs
    negatives = jnp.sum(jnp.where(real, picked, 0.0), axis=-1, keepdims=True)
    loss = jnp.log(jnp.exp(positive) + negatives) - positive
    starts = starts_ref[pl.ds(lax.axis_index("tensor"), 1), :]
    o_ref[...] = jnp.where(frame_mask(starts, lax.axis_index("seq") * frames, frames) > 0, loss, 0.0)


def losses(powers, positive, ids, starts):
    return pl.pallas_call(
        loss_body,
        out_shape=jax.ShapeDtypeStruct((ids.shape[0], 1), jnp.float32),
        scratch_shapes=[pltpu.VMEM((ids.shape[0], LANES), jnp.int32)],
        compiler_params=pltpu.CompilerParams(vmem_limit_bytes=24 * 2**20),
    )(powers, positive, ids, starts)


def on_device(
    feature_in,
    conv_weight,
    proj_weight,
    mask_embed,
    pos_weight,
    final_weight,
    codebook,
    quant_weight,
    mask_starts,
    code_choice,
    negative_ids,
):
    sizes = tuple(lax.axis_size(name) for name in ("dp", "seq", "tensor"))
    powers, positive = main_stage(
        sizes,
        feature_in,
        conv_weight,
        proj_weight.T,
        mask_embed.reshape(1, -1),
        mask_starts,
        codebook,
        quant_weight,
        final_weight.reshape(2, -1, final_weight.shape[1]),
        pos_weight,
        code_choice[0].T,
    )
    loss = losses(powers, positive, negative_ids[0], mask_starts)
    return loss.reshape(1, -1)


def solution(mesh):
    return jax.shard_map(
        on_device,
        mesh=mesh,
        in_specs=(
            P("dp", "seq", "tensor"),
            P(None, "tensor", None),
            P(None, "tensor"),
            P("tensor"),
            P(("dp", "seq"), "tensor", None, None),
            P("tensor", None),
            P(),
            P(),
            P("dp", None),
            P(("dp", "tensor"), "seq", None),
            P(("dp", "tensor"), "seq", None),
        ),
        out_specs=P(("dp", "tensor"), "seq"),
        check_vma=False,
    )
```

```python
import functools

import jax
import jax.numpy as jnp
from jax import lax
from jax.experimental import pallas as pl
from jax.experimental.pallas import tpu as pltpu
from jax.sharding import PartitionSpec as P

KERNEL = 128
MASK_LEN = 10
SHIFTS = 16
LANES = 128


ln_eps = 1e-05
norm_eps = 1e-06
logit_temp = 0.1


def exact_gelu(value):
    return 0.5 * value * (1.0 + lax.erf(value * (0.5**0.5)))


def remote(src, dst, send, recv, **coords):
    return pltpu.make_async_remote_copy(
        src_ref=src,
        dst_ref=dst,
        send_sem=send,
        recv_sem=recv,
        device_id=coords,
        device_id_type=pl.DeviceIdType.MESH,
    )


def greet(barrier, **coords):
    pl.semaphore_signal(
        barrier, inc=1, device_id=coords, device_id_type=pl.DeviceIdType.MESH
    )


def frame_mask(starts, first, frames):
    position = first + lax.broadcasted_iota(jnp.int32, (frames, starts.shape[1]), 0)
    inside = (position >= starts) & (position < starts + MASK_LEN)
    return jnp.max(jnp.where(inside, 1.0, 0.0), axis=-1, keepdims=True)


def main_body(
    sizes,
    x_hbm,
    cw_hbm,
    pw_hbm,
    embed_hbm,
    starts_hbm,
    book_hbm,
    qw_hbm,
    fw_hbm,
    taps_in,
    codes_in,
    powers_ref,
    positive_ref,
    targets_ref,
    norms_ref,
    x_in,
    cw_ref,
    pw_ref,
    embed_ref,
    starts_ref,
    book_ref,
    qw_ref,
    fw_ref,
    taps_ref,
    codes_ref,
    choice,
    codevec,
    x_wide,
    term_wide,
    term_half,
    arrived,
    feat,
    hidden,
    win_ref,
    xf,
    xc,
    wc,
    acc,
    mixed,
    gathered,
    joined,
    load_sem,
    local_sem,
    code_send,
    code_recv,
    tap_send,
    tap_recv,
    ring_send,
    ring_recv,
    pair_send,
    pair_recv,
    sum_send,
    sum_recv,
    feat_send,
    feat_recv,
    win_send,
    win_recv,
    mix_send,
    mix_recv,
    final_send,
    final_recv,
    side_send,
    side_recv,
):
    dps, seqs, tensors = sizes
    chips = seqs // 2
    dp, seq, tensor = (lax.axis_index(name) for name in ("dp", "seq", "tensor"))
    utts, frames, channels = term_wide.shape
    inner = taps_ref.shape[-1]

    def other_dp(k):
        return lax.rem(dp + k, dps)

    def other_seq(k):
        return lax.rem(seq + (k + seqs) % seqs, seqs)

    def other_tensor(k):
        return lax.rem(tensor + k, tensors)

    loads = [
        pltpu.make_async_copy(source, target, load_sem.at[index])
        for index, (source, target) in enumerate(
            (
                (x_hbm, x_in),
                (cw_hbm, cw_ref),
                (pw_hbm, pw_ref),
                (embed_hbm, embed_ref),
                (starts_hbm, starts_ref),
                (book_hbm, book_ref),
                (qw_hbm, qw_ref),
            )
        )
    ]
    for copy in loads:
        copy.start()
    local = pltpu.make_async_copy(taps_in.at[:, dp], taps_ref.at[dp, seq], local_sem.at[0])
    local.start()
    local_codes = pltpu.make_async_copy(codes_in, codes_ref.at[seq], local_sem.at[1])
    local_codes.start()
    local_final = pltpu.make_async_copy(fw_hbm, fw_ref.at[tensor], local_sem.at[2])
    local_final.start()

    barrier = pltpu.get_barrier_semaphore()
    for k in range(1, seqs):
        greet(barrier, seq=other_seq(k))
    for k in range(1, dps):
        for side in (-1, 0, 1):
            greet(barrier, dp=other_dp(k), seq=other_seq(side))
    for k in range(1, tensors):
        for m in range(dps):
            greet(barrier, tensor=other_tensor(k), dp=other_dp(m))
    pl.semaphore_wait(barrier, (seqs - 1) + 3 * (dps - 1) + (tensors - 1) * dps)

    pending = []

    def begin(copy):
        copy.start()
        pending.append(copy)
        return copy

    tap_copies = [
        begin(
            remote(
                taps_in.at[:, other_dp(k)],
                taps_ref.at[dp, seq],
                tap_send.at[k - 1],
                tap_recv.at[k - 1],
                dp=other_dp(k),
            )
        )
        for k in range(1, dps)
    ]
    code_copies = [
        begin(
            remote(
                codes_in,
                codes_ref.at[seq],
                code_send.at[k - 1],
                code_recv.at[k - 1],
                seq=other_seq(k),
            )
        )
        for k in range(1, seqs)
    ]

    loads[0].wait()
    loads[1].wait()
    x_wide[...] = x_in[...].reshape(x_wide.shape).astype(jnp.float32)
    term = jnp.zeros((utts * frames, channels), jnp.float32)
    for tap in range(2):
        rows = x_wide[pl.ds(tap, utts * frames, stride=2), :].astype(jnp.bfloat16)
        term += jnp.dot(rows, cw_ref[tap], preferred_element_type=jnp.float32)
    term = term.reshape(utts, frames, channels)
    term_wide[...] = term
    term_half[...] = term.astype(jnp.bfloat16)
    sum_copies = [
        begin(
            remote(
                term_half.at[other_tensor(k)],
                arrived.at[k - 1],
                sum_send.at[k - 1],
                sum_recv.at[k - 1],
                tensor=other_tensor(k),
            )
        )
        for k in range(1, tensors)
    ]

    local.wait()
    for copy in tap_copies:
        copy.wait_recv()

    core = lax.rem(seq, 2)
    sibling = seq + 1 - 2 * core
    ups, downs = chips // 2, (chips - 1) // 2
    split = dps // 2

    def block_of(hop, part):
        index = lax.rem(seq + 2 * hop + seqs, seqs)
        if part is None:
            return taps_ref.at[:, index]
        return taps_ref.at[pl.ds(part * split, split), index]

    def pass_block(slot, hop, part=None):
        block = block_of(hop, part)
        return begin(
            remote(block, block, pair_send.at[slot], pair_recv.at[slot], seq=sibling)
        )

    def ring(slot, hop, direction, part=None):
        block = block_of(hop, part)
        return begin(
            remote(
                block,
                block,
                ring_send.at[slot],
                ring_recv.at[slot],
                seq=other_seq(2 * direction),
            )
        )

    up = [ring(0, 0, 1)]
    down = [ring(ups, 0, -1)]
    passed = {0: [pass_block(0, 0)]}

    def advance(step):
        last = step == ups
        up[step - 1].wait_recv()
        if not last:
            up.append(ring(step, -step, 1, 0 if step == ups - 1 else None))
        down[step - 1].wait_recv()
        if not last:
            down.append(ring(ups + step, step, -1, 1 if step == ups - 1 else None))
        if last:
            passed[-step] = [pass_block(step, -step, 0), pass_block(ups + step, -step, 1)]
        else:
            passed[-step] = [pass_block(step, -step)]
            passed[step] = [pass_block(ups + step, step)]

    for copy in loads[2:]:
        copy.wait()
    local_codes.wait()
    for copy in code_copies:
        copy.wait_recv()
    for block in range(seqs):
        choice[:, block * frames : (block + 1) * frames] = codes_ref[block]
    entries, width = book_ref.shape[1:]
    half = choice.shape[1] // 2

    def make_targets(part):
        here = slice(part * half, (part + 1) * half)
        for qgroup in range(book_ref.shape[0]):
            row = lax.broadcasted_iota(jnp.int32, (entries, half), 0)
            onehot = jnp.where(row == choice[qgroup : qgroup + 1, here], 1.0, 0.0)
            codevec[:, qgroup * width : (qgroup + 1) * width] = lax.dot_general(
                onehot.astype(jnp.bfloat16),
                book_ref[qgroup],
                (((0,), (0,)), ((), ())),
                preferred_element_type=jnp.float32,
            ).astype(jnp.bfloat16)
        made = jnp.dot(codevec[...], qw_ref[...], preferred_element_type=jnp.float32)
        made = made.astype(jnp.bfloat16)
        targets_ref[here, :] = made
        made = made.astype(jnp.float32)
        norm = jnp.sum(made * made, axis=-1, keepdims=True)
        norms_ref[:, here] = jnp.transpose(jnp.broadcast_to(norm, (half, LANES)))[:1]

    make_targets(0)
    summed = term_wide[tensor]
    for k, copy in enumerate(sum_copies):
        copy.wait_recv()
        summed = summed + arrived[k].astype(jnp.float32)
    row_mean = jnp.mean(summed, axis=-1, keepdims=True)
    row_square = jnp.mean(summed * summed, axis=-1, keepdims=True)
    normed = (summed - row_mean) * lax.rsqrt(row_square - row_mean * row_mean + ln_eps)
    feat[tensor] = exact_gelu(normed).astype(jnp.bfloat16)
    feat_copies = [
        begin(
            remote(
                feat.at[tensor],
                feat.at[tensor],
                feat_send.at[k - 1],
                feat_recv.at[k - 1],
                tensor=other_tensor(k),
            )
        )
        for k in range(1, tensors)
    ]
    final_copies = [
        begin(
            remote(
                fw_hbm.at[core],
                fw_ref.at[tensor, core],
                final_send.at[k - 1],
                final_recv.at[k - 1],
                tensor=other_tensor(k),
            )
        )
        for k in range(1, tensors)
    ]
    make_targets(1)
    advance(1)
    is_masked = (
        jnp.concatenate(
            [frame_mask(starts_ref[u : u + 1], seq * frames, frames) for u in range(utts)], axis=0
        )
        > 0
    )
    for copy in feat_copies:
        copy.wait_recv()
    features = feat[...].reshape(utts * frames, channels)
    embed = embed_ref[...].astype(jnp.float32)
    hidden[...] = jnp.zeros_like(hidden)
    for group in range(dps):
        here = slice(group * inner, (group + 1) * inner)
        projected = lax.dot_general(
            features,
            pw_ref[here, :],
            (((1,), (1,)), ((), ())),
            preferred_element_type=jnp.float32,
        )
        chosen = jnp.where(is_masked, embed[:, here], projected)
        hidden[group, :, :, :inner] = chosen.astype(jnp.bfloat16).reshape(utts, frames, inner)
    mine = pl.ds(dp * utts, utts)
    win_copies = []
    for k in range(dps):
        for side in (-1, 0, 1):
            slot = 3 * k + side + 1
            if k == 0 and side == 0:
                continue
            win_copies.append(
                begin(
                    remote(
                        hidden.at[other_dp(k)],
                        win_ref.at[mine, 1 - side],
                        win_send.at[slot],
                        win_recv.at[slot],
                        dp=other_dp(k),
                        seq=other_seq(side),
                    )
                )
            )
    win_ref[mine, 1] = hidden[dp]
    advance(2)
    for copy in win_copies:
        copy.wait_recv()

    @pl.when(seq == 0)
    def low_edge():
        win_ref[:, 0] = jnp.zeros_like(win_ref[:, 0])

    @pl.when(seq == seqs - 1)
    def high_edge():
        win_ref[:, 2] = jnp.zeros_like(win_ref[:, 2])

    kept = xc.shape[1]
    acc[...] = jnp.zeros_like(acc)
    wc[...] = jnp.zeros_like(wc)

    @pl.loop(0, dps * utts)
    def shift_copies(u):
        xf[...] = win_ref[u].reshape(xf.shape).astype(jnp.float32)
        for j in range(SHIFTS):
            xc[u, :, j * LANES : (j + 1) * LANES] = xf[j : j + kept, :].astype(jnp.bfloat16)

    span = acc.shape[1]
    run = wc.shape[1]

    def load_block(hop):
        for copy in passed[hop]:
            copy.wait_recv()
        chip = lax.div(lax.rem(seq - core + 2 * hop + seqs, seqs), 2)
        lane = pl.multiple_of(lax.rem(chip, 4) * run, run)
        base = lax.div(chip, 4) * SHIFTS
        for pair in range(dps // 2):
            for side in range(2):
                for i in range(4):
                    wc[
                        pair, i * LANES : i * LANES + inner, side * LANES : side * LANES + inner
                    ] = taps_ref[2 * pair + side, 2 * chip + i // 2, i % 2]
        return lane, base

    def chunk_total(chunk, lane, base):
        here = pl.ds(chunk * utts, utts)
        total = acc[here]
        for pair in range(dps // 2):
            first = pl.multiple_of(base + 64 * pair, SHIFTS)
            window = xc[here, pl.ds(first, span), pl.ds(lane, run)]
            total += jnp.dot(
                window.reshape(utts * span, run),
                wc[pair],
                preferred_element_type=jnp.float32,
            ).reshape(utts, span, 2 * LANES)
        return total

    def conv_block(hop):
        lane, base = load_block(hop)

        @pl.loop(0, dps)
        def multiply(chunk):
            acc[pl.ds(chunk * utts, utts)] = chunk_total(chunk, lane, base)

    conv_block(0)
    advance(3)
    conv_block(1)
    conv_block(-1)
    conv_block(2)
    conv_block(-2)
    advance(4)
    final_passes = []
    for k, copy in enumerate(final_copies):
        copy.wait_recv()
        block = fw_ref.at[lax.rem(tensor + tensors - k - 1, tensors), core]
        final_passes.append(
            begin(remote(block, block, side_send.at[k], side_recv.at[k], seq=sibling))
        )
    conv_block(3)
    conv_block(-3)

    lane, base = load_block(-4)
    mix_copies = []
    for k in (1, 2, 3, 0):
        chunk = other_dp(k)
        total = chunk_total(chunk, lane, base)
        conv_out = total[:, :frames, :LANES] + total[:, span - frames :, LANES:]
        own = win_ref[pl.ds(chunk * utts, utts), 1].astype(jnp.float32)
        mixed[pl.ds(chunk * utts, utts)] = (own + exact_gelu(conv_out)).astype(jnp.bfloat16)
        for m in (2, 1, 3, 0):
            if k == 0 and m == 0:
                continue
            slot = k * tensors + m
            mix_copies.append(
                begin(
                    remote(
                        mixed.at[chunk * utts + other_tensor(m)],
                        gathered.at[tensor * dps + dp],
                        mix_send.at[slot],
                        mix_recv.at[slot],
                        dp=chunk,
                        tensor=other_tensor(m),
                    )
                )
            )
    gathered[tensor * dps + dp] = mixed[dp * utts + tensor]
    local_final.wait()
    for copy in final_passes + mix_copies:
        copy.wait_recv()
    code_dim = fw_ref.shape[-1]
    for group in range(tensors * dps):
        joined[:, group * inner : (group + 1) * inner] = gathered[group][:, :inner]
    total = jnp.dot(
        joined[...],
        fw_ref[...].reshape(joined.shape[1], code_dim),
        preferred_element_type=jnp.float32,
    )
    context = total.astype(jnp.bfloat16)
    scores = lax.dot_general(
        context,
        targets_ref[...],
        (((1,), (1,)), ((), ())),
        preferred_element_type=jnp.float32,
    )
    wide = context.astype(jnp.float32)
    first = pl.multiple_of(seq * frames, frames)
    own = targets_ref[pl.ds(first, frames), :].astype(jnp.float32)
    ctx_norm = jnp.sum(wide * wide, axis=-1, keepdims=True) + norm_eps
    own_norm = jnp.sum(own * own, axis=-1, keepdims=True) + norm_eps
    pos_dot = jnp.sum(wide * own, axis=-1, keepdims=True)
    positive_ref[...] = pos_dot * lax.rsqrt(ctx_norm * own_norm) / logit_temp
    logits = scores * lax.rsqrt(ctx_norm * (norms_ref[...] + norm_eps)) / logit_temp
    powers_ref[...] = jnp.exp(logits)
    for copy in pending:
        copy.wait_send()


def main_stage(sizes, x, cw, pw, embed, starts, book, qw, fw, taps, codes):
    dps, seqs, tensors = sizes
    utts, frames = x.shape[0], x.shape[1] // 2
    channels = cw.shape[2]
    code_dim = fw.shape[2]
    per, _, inner, outer = taps.shape
    hops = seqs // 2
    span = frames + KERNEL // dps
    hbm = pl.BlockSpec(memory_space=pltpu.HBM)
    vmem = pl.BlockSpec(memory_space=pltpu.VMEM)
    dma = pltpu.SemaphoreType.DMA
    half = jnp.bfloat16

    def like(array):
        return pltpu.VMEM(array.shape, array.dtype)

    return pl.pallas_call(
        functools.partial(main_body, sizes),
        out_shape=(
            jax.ShapeDtypeStruct((frames, seqs * frames), jnp.float32),
            jax.ShapeDtypeStruct((frames, 1), jnp.float32),
        ),
        in_specs=[hbm] * 10,
        out_specs=(vmem, vmem),
        scratch_shapes=[
            pltpu.VMEM((seqs * frames, code_dim), half),
            pltpu.VMEM((1, seqs * frames), jnp.float32),
            like(x),
            like(cw),
            like(pw),
            like(embed),
            like(starts),
            like(book),
            like(qw),
            pltpu.VMEM((tensors,) + fw.shape, half),
            pltpu.VMEM((dps, seqs, per, inner, outer), half),
            pltpu.VMEM((seqs,) + codes.shape, codes.dtype),
            pltpu.VMEM((codes.shape[0], seqs * frames), codes.dtype),
            pltpu.VMEM((seqs * frames // 2, qw.shape[0]), half),
            pltpu.VMEM((2 * utts * frames, x.shape[2]), jnp.float32),
            pltpu.VMEM((utts, frames, channels), jnp.float32),
            pltpu.VMEM((utts, frames, channels), half),
            pltpu.VMEM((tensors - 1, frames, channels), half),
            pltpu.VMEM((utts, frames, channels), half),
            pltpu.VMEM((dps, utts, frames, LANES), half),
            pltpu.VMEM((utts * dps, 3, frames, LANES), half),
            pltpu.VMEM((3 * frames, LANES), jnp.float32),
            pltpu.VMEM((utts * dps, 3 * frames - SHIFTS, SHIFTS * LANES), half),
            pltpu.VMEM((dps // 2, 4 * LANES, 2 * LANES), half),
            pltpu.VMEM((utts * dps, span, 2 * LANES), jnp.float32),
            pltpu.VMEM((utts * dps, frames, LANES), half),
            pltpu.VMEM((tensors * dps, frames, LANES), half),
            pltpu.VMEM((frames, tensors * dps * inner), half),
            dma((7,)),
            dma((3,)),
            dma((seqs - 1,)),
            dma((seqs - 1,)),
            dma((dps - 1,)),
            dma((dps - 1,)),
            dma((hops,)),
            dma((hops,)),
            dma((hops + 1,)),
            dma((hops + 1,)),
            dma((tensors - 1,)),
            dma((tensors - 1,)),
            dma((tensors - 1,)),
            dma((tensors - 1,)),
            dma((3 * dps,)),
            dma((3 * dps,)),
            dma((dps * tensors,)),
            dma((dps * tensors,)),
            dma((tensors - 1,)),
            dma((tensors - 1,)),
            dma((tensors - 1,)),
            dma((tensors - 1,)),
        ],
        compiler_params=pltpu.CompilerParams(
            collective_id=0, has_side_effects=True, vmem_limit_bytes=60 * 2**20
        ),
    )(x, cw, pw, embed, starts, book, qw, fw, taps, codes)


def loss_body(powers_ref, positive_ref, ids_ref, starts_ref, o_ref, ids):
    frames, negs = ids_ref.shape
    ids[...] = jnp.zeros_like(ids)
    ids[:, :negs] = ids_ref[...]
    powers = powers_ref[...]
    positive = positive_ref[...]
    chosen = ids[...]
    lane = chosen % LANES
    chunk = chosen // LANES
    picked = jnp.zeros((frames, LANES), jnp.float32)
    for c in range(powers.shape[1] // LANES):
        found = jnp.take_along_axis(
            powers[:, c * LANES : (c + 1) * LANES], lane, axis=1, mode="promise_in_bounds"
        )
        picked = jnp.where(chunk == c, found, picked)
    real = lax.broadcasted_iota(jnp.int32, picked.shape, 1) < negs
    negatives = jnp.sum(jnp.where(real, picked, 0.0), axis=-1, keepdims=True)
    loss = jnp.log(jnp.exp(positive) + negatives) - positive
    starts = starts_ref[pl.ds(lax.axis_index("tensor"), 1), :]
    o_ref[...] = jnp.where(frame_mask(starts, lax.axis_index("seq") * frames, frames) > 0, loss, 0.0)


def losses(powers, positive, ids, starts):
    return pl.pallas_call(
        loss_body,
        out_shape=jax.ShapeDtypeStruct((ids.shape[0], 1), jnp.float32),
        scratch_shapes=[pltpu.VMEM((ids.shape[0], LANES), jnp.int32)],
        compiler_params=pltpu.CompilerParams(vmem_limit_bytes=24 * 2**20),
    )(powers, positive, ids, starts)


def on_device(
    feature_in,
    conv_weight,
    proj_weight,
    mask_embed,
    pos_weight,
    final_weight,
    codebook,
    quant_weight,
    mask_starts,
    code_choice,
    negative_ids,
):
    sizes = tuple(lax.axis_size(name) for name in ("dp", "seq", "tensor"))
    powers, positive = main_stage(
        sizes,
        feature_in,
        conv_weight,
        proj_weight.T,
        mask_embed.reshape(1, -1),
        mask_starts,
        codebook,
        quant_weight,
        final_weight.reshape(2, -1, final_weight.shape[1]),
        pos_weight,
        code_choice[0].T,
    )
    loss = losses(powers, positive, negative_ids[0], mask_starts)
    return loss.reshape(1, -1)


def solution(mesh):
    return jax.shard_map(
        on_device,
        mesh=mesh,
        in_specs=(
            P("dp", "seq", "tensor"),
            P(None, "tensor", None),
            P(None, "tensor"),
            P("tensor"),
            P(("dp", "seq"), "tensor", None, None),
            P("tensor", None),
            P(),
            P(),
            P("dp", None),
            P(("dp", "tensor"), "seq", None),
            P(("dp", "tensor"), "seq", None),
        ),
        out_specs=P(("dp", "tensor"), "seq"),
        check_vma=False,
    )
```
